32 devices in a mesh: dp: 8 (over y, x, core), ctx: 4 (over z).
Axes of the slice: x: 2, y: 2, z: 4, core: 2. Of those that a mesh axis runs over, the one named last changes fastest.
Arguments:
- layer_input: bfloat16 [4096, 2048], P(('dp', 'ctx')), may hold values from -6 to 6
- block_table: int32 [8, 4], P('dp'), may hold values from 0 to 3, as said below
- positions: int32 [4096], P(('dp', 'ctx')), may hold values from 0 to 511, as said below
- first_gain: float32 [2048], P(('dp', 'ctx')), may hold values from 0.25 to 1.75
- first_shift: float32 [2048], P(('dp', 'ctx')), may hold values from -3 to 3
- qkv_weight: bfloat16 [2048, 6144], P(('dp', 'ctx')), may hold values from -0.125 to 0.125
- qkv_bias: float32 [6144], P(('dp', 'ctx')), may hold values from -3 to 3
- out_weight: bfloat16 [2048, 2048], P(('dp', 'ctx')), may hold values from -0.5 to 0.5
- second_gain: float32 [2048], P(('dp', 'ctx')), may hold values from 0.25 to 1.75
- second_shift: float32 [2048], P(('dp', 'ctx')), may hold values from -3 to 3
- gate_weight: bfloat16 [2048, 5632], P(('dp', 'ctx')), may hold values from -0.125 to 0.125
- up_weight: bfloat16 [2048, 5632], P(('dp', 'ctx')), may hold values from -0.125 to 0.125
- down_weight: bfloat16 [5632, 2048], P(('dp', 'ctx')), may hold values from -0.078125 to 0.078125
- cotangent: bfloat16 [4096, 2048], P(('dp', 'ctx')), may hold values from -6 to 6
Outputs:
- layer_output: bfloat16 [4096, 2048], P(('dp', 'ctx'))
- grad_input: float32 [4096, 2048], P(('dp', 'ctx'))
- grad_first_gain: float32 [2048], P(('dp', 'ctx'))
- grad_first_shift: float32 [2048], P(('dp', 'ctx'))
- grad_qkv_weight: float32 [2048, 6144], P(('dp', 'ctx'))
- grad_qkv_bias: float32 [6144], P(('dp', 'ctx'))
- grad_out_weight: float32 [2048, 2048], P(('dp', 'ctx'))
- grad_second_gain: float32 [2048], P(('dp', 'ctx'))
- grad_second_shift: float32 [2048], P(('dp', 'ctx'))
- grad_gate_weight: float32 [2048, 5632], P(('dp', 'ctx'))
- grad_up_weight: float32 [2048, 5632], P(('dp', 'ctx'))
- grad_down_weight: float32 [5632, 2048], P(('dp', 'ctx'))
The draws below stay inside these ranges and needn't reach their ends.
Inputs may be any that keep to these rules, and one draw needn't show every extreme that they name: `block_table`: row g lists, for the blocks of group g in device order, their block numbers in the group's logical order; each row is a permutation. `positions`: put in logical order, each group's 512 tokens are one or two whole sequences laid end to end, and a token's position is its index within its sequence.
All inputs are finite; a program needn't handle non-finite values.
Results may differ from the reference program's by a relative error of at most 0.035.
Values may be sent and summed in bfloat16 or wider, within the bound.
No kernel may reach another device: no remote copies, remote signals or barrier semaphores. Data moves between devices by JAX's collectives and lax.ppermute only.
A program may use at most 256 MiB of HBM per device.

```python
import jax
import jax.numpy as jnp
from jax import lax

D = 2048
H = 32
HD = 64
ROT = 16
FF = 5632
BLOCK = 128
GROUP_BLOCKS = 4
GROUP_TOK = 512
GROUPS = 8
TOKENS = 4096


def group_layout(key, group):
    group_key = jax.random.fold_in(key, group)
    order_key, start_key = jax.random.split(group_key)
    table_row = jax.random.permutation(order_key, GROUP_BLOCKS).astype(jnp.int32)
    counter = jnp.arange(GROUP_TOK, dtype=jnp.int32)
    split = jax.random.randint(start_key, (), 1, GROUP_TOK)
    starts = (counter == 0) | (counter == split) & (group != 0)
    first = lax.cummax(jnp.where(starts, counter, 0), axis=0)
    logical_pos = counter - first
    device_pos = logical_pos.reshape(GROUP_BLOCKS, BLOCK)[table_row].reshape(GROUP_TOK)
    return (table_row, device_pos.astype(jnp.int32))


def whole_layout(key):
    layout_key = jax.random.fold_in(key, 7)
    groups_here = jnp.arange(GROUPS, dtype=jnp.int32)
    return jax.vmap(lambda group: group_layout(layout_key, group))(groups_here)


def draw_block_table(key, part):
    return whole_layout(key)[0]


def draw_positions(key, part):
    return whole_layout(key)[1].reshape(TOKENS)


def levels(key, extent, cuts, low, high):
    def one(axis_at, shards_of):
        steps = jax.random.uniform(jax.random.fold_in(jax.random.fold_in(key, 6), axis_at), (shards_of,), jnp.float32, low / len(cuts), high / len(cuts))
        return jnp.repeat(jnp.exp(steps), extent[axis_at] // shards_of).reshape((-1,) + (1,) * (len(extent) - axis_at - 1))

    level = one(*cuts[0])
    for cut in cuts[1:]:
        level = level * one(*cut)
    return level


def noise(key, extent, width, limit, shards=(), held_as=jnp.bfloat16):
    level = levels(key, extent, shards, -0.22, 0.18) if shards else 1.0
    array = jax.random.normal(key, extent, jnp.float32) * width * level
    return jnp.minimum(jnp.maximum(array, -limit), limit).astype(held_as)


def setup_inputs(seed: int = 0) -> dict:
    arg_keys = jax.random.split(jax.random.key(seed), 15)
    return {
        "layer_input": noise(arg_keys[0], (TOKENS, D), 1.0, 6.0, ((0, 32),)),
        "block_table": draw_block_table(jax.random.fold_in(arg_keys[14], 71), 0),
        "positions": draw_positions(jax.random.fold_in(arg_keys[14], 71), 0),
        "first_gain": jnp.clip(1.0 + 0.15 * jax.random.normal(arg_keys[3], (D,), jnp.float32), 0.25, 1.75),
        "first_shift": noise(arg_keys[4], (D,), 0.5, 3.0, ((0, 32),), jnp.float32),
        "qkv_weight": noise(arg_keys[5], (D, 3 * D), D ** -0.5, 0.125, ((0, 32),)),
        "qkv_bias": noise(arg_keys[6], (3 * D,), 0.5, 3.0, ((0, 32),), jnp.float32),
        "out_weight": noise(arg_keys[7], (D, D), (D // 16) ** -0.5, 0.5, ((0, 32),)),
        "second_gain": jnp.clip(1.0 + 0.15 * jax.random.normal(arg_keys[8], (D,), jnp.float32), 0.25, 1.75),
        "second_shift": noise(arg_keys[9], (D,), 0.5, 3.0, ((0, 32),), jnp.float32),
        "gate_weight": noise(arg_keys[10], (D, FF), D ** -0.5, 0.125, ((0, 32),)),
        "up_weight": noise(arg_keys[11], (D, FF), D ** -0.5, 0.125, ((0, 32),)),
        "down_weight": noise(arg_keys[12], (FF, D), FF ** -0.5, 0.078125, ((0, 32),)),
        "cotangent": noise(arg_keys[13], (TOKENS, D), 1.0, 6.0, ((0, 32),)),
    }


EPS = 1e-05

def layer_norm(values, gain, shift):
    average = lax.optimization_barrier(jnp.mean(values, axis=-1, keepdims=True))
    centred = values - average
    inverse = lax.rsqrt(lax.optimization_barrier(jnp.mean(centred * centred, axis=-1, keepdims=True)) + EPS)
    normed = centred * inverse
    return (normed * gain + shift, normed, inverse)

def norm_back(upstream, gain, normed, inverse):
    scaled = upstream * gain
    centred = scaled - lax.optimization_barrier(jnp.mean(scaled, axis=-1, keepdims=True))
    return inverse * (centred - normed * lax.optimization_barrier(jnp.mean(scaled * normed, axis=-1, keepdims=True)))

def rotary_tables(token_pos):
    half_rot = ROT // 2
    freqs = 10000.0 ** (-2.0 * jnp.arange(half_rot, dtype=jnp.float32) / ROT)
    angles = token_pos.astype(jnp.float32)[:, None] * freqs[None, :]
    return (jnp.cos(angles)[:, None, :], jnp.sin(angles)[:, None, :])

def rotate(field, cosine, sine):
    half_rot = ROT // 2
    first = field[..., :half_rot]
    second = field[..., half_rot:ROT]
    return jnp.concatenate([first * cosine - second * sine, second * cosine + first * sine, field[..., ROT:]], axis=-1)

def logical_index(table_row):
    offsets = jnp.tile(jnp.arange(BLOCK, dtype=jnp.int32), table_row.shape[0])
    return (jnp.repeat(table_row, BLOCK) * BLOCK + offsets).astype(jnp.int32)

def reference(layer_input, block_table, positions, first_gain, first_shift, qkv_weight, qkv_bias, out_weight, second_gain, second_shift, gate_weight, up_weight, down_weight, cotangent):
    scale = HD ** (-0.5)
    inputs_all = layer_input.reshape(GROUPS, GROUP_TOK, D)
    cot_all = cotangent.reshape(GROUPS, GROUP_TOK, D)
    pos_all = positions.reshape(GROUPS, GROUP_TOK)

    def one_group(totals, pieces):
        x_group, cot_group, pos_group, table_row = pieces
        count = x_group.shape[0]
        index_all = logical_index(table_row)
        visible = (index_all[None, :] <= index_all[:, None]) & (index_all[None, :] >= index_all[:, None] - pos_group[:, None])
        visible = visible[None]
        inputs = x_group.astype(jnp.float32)
        norm_one, normed_one, inverse_one = layer_norm(inputs, first_gain, first_shift)
        norm_one_b = norm_one.astype(jnp.bfloat16)
        proj = jnp.dot(norm_one_b, qkv_weight, preferred_element_type=jnp.float32)
        query = proj[:, :D] + qkv_bias[:D]
        keyproj = proj[:, D:2 * D] + qkv_bias[D:2 * D]
        value = proj[:, 2 * D:] + qkv_bias[2 * D:]
        cosine, sine = rotary_tables(pos_group)
        query_rot = rotate(query.reshape(count, H, HD), cosine, sine).astype(jnp.bfloat16)
        key_rot = rotate(keyproj.reshape(count, H, HD), cosine, sine).astype(jnp.bfloat16)
        value_b = value.reshape(count, H, HD).astype(jnp.bfloat16)
        scores = jnp.einsum('qhd,khd->hqk', query_rot.astype(jnp.float32), key_rot.astype(jnp.float32)) * scale
        log_total = jnp.log(lax.optimization_barrier(jnp.sum(jnp.where(visible, jnp.exp(scores), 0.0), axis=-1)))
        prob = jnp.where(visible, jnp.exp(scores - log_total[..., None]), 0.0)
        prob_b = prob.astype(jnp.bfloat16)
        attended = jnp.einsum('hqk,khd->qhd', prob_b.astype(jnp.float32), value_b.astype(jnp.float32)).astype(jnp.bfloat16)
        attended_flat = attended.reshape(count, D)
        mixed = inputs + jnp.dot(attended_flat, out_weight, preferred_element_type=jnp.float32)
        norm_two, normed_two, inverse_two = layer_norm(mixed, second_gain, second_shift)
        norm_two_b = norm_two.astype(jnp.bfloat16)
        gate = jnp.dot(norm_two_b, gate_weight, preferred_element_type=jnp.float32)
        upval = jnp.dot(norm_two_b, up_weight, preferred_element_type=jnp.float32)
        sigma = jax.nn.sigmoid(gate)
        act_b = (gate * sigma * upval).astype(jnp.bfloat16)
        output = (mixed + jnp.dot(act_b, down_weight, preferred_element_type=jnp.float32)).astype(jnp.bfloat16)
        upstream = cot_group.astype(jnp.float32)
        grad_down = jnp.dot(act_b.T, cot_group, preferred_element_type=jnp.float32)
        grad_act = jnp.dot(cot_group, down_weight.T, preferred_element_type=jnp.float32)
        grad_gate_b = (grad_act * upval * sigma * (1.0 + gate * (1.0 - sigma))).astype(jnp.bfloat16)
        grad_up_b = (grad_act * gate * sigma).astype(jnp.bfloat16)
        grad_gate_w = jnp.dot(norm_two_b.T, grad_gate_b, preferred_element_type=jnp.float32)
        grad_up_w = jnp.dot(norm_two_b.T, grad_up_b, preferred_element_type=jnp.float32)
        grad_norm_two = jnp.dot(grad_gate_b, gate_weight.T, preferred_element_type=jnp.float32) + jnp.dot(grad_up_b, up_weight.T, preferred_element_type=jnp.float32)
        grad_gain_two = lax.optimization_barrier(jnp.sum(grad_norm_two * normed_two, axis=0))
        grad_shift_two = lax.optimization_barrier(jnp.sum(grad_norm_two, axis=0))
        grad_mixed = upstream + norm_back(grad_norm_two, second_gain, normed_two, inverse_two)
        grad_mixed_b = grad_mixed.astype(jnp.bfloat16)
        grad_out_w = jnp.dot(attended_flat.T, grad_mixed_b, preferred_element_type=jnp.float32)
        grad_att = jnp.dot(grad_mixed_b, out_weight.T, preferred_element_type=jnp.float32).astype(jnp.bfloat16).reshape(count, H, HD)
        grad_value = jnp.einsum('hqk,qhd->khd', prob_b.astype(jnp.float32), grad_att.astype(jnp.float32))
        grad_prob = jnp.einsum('qhd,khd->hqk', grad_att.astype(jnp.float32), value_b.astype(jnp.float32))
        delta = lax.optimization_barrier(jnp.sum(grad_att.astype(jnp.float32) * attended.astype(jnp.float32), axis=-1)).T
        grad_scores = (prob * (grad_prob - delta[..., None]) * scale).astype(jnp.bfloat16)
        grad_query = jnp.einsum('hqk,khd->qhd', grad_scores.astype(jnp.float32), key_rot.astype(jnp.float32))
        grad_key = jnp.einsum('hqk,qhd->khd', grad_scores.astype(jnp.float32), query_rot.astype(jnp.float32))
        grad_query = rotate(grad_query, cosine, -sine).reshape(count, D)
        grad_key = rotate(grad_key, cosine, -sine).reshape(count, D)
        grad_value = grad_value.reshape(count, D)
        grad_bias = jnp.concatenate([lax.optimization_barrier(jnp.sum(grad_query, axis=0)), lax.optimization_barrier(jnp.sum(grad_key, axis=0)), lax.optimization_barrier(jnp.sum(grad_value, axis=0))])
        grad_proj_b = jnp.concatenate([grad_query, grad_key, grad_value], axis=-1).astype(jnp.bfloat16)
        grad_qkv_w = jnp.dot(norm_one_b.T, grad_proj_b, preferred_element_type=jnp.float32)
        grad_norm_one = jnp.dot(grad_proj_b, qkv_weight.T, preferred_element_type=jnp.float32)
        grad_gain_one = lax.optimization_barrier(jnp.sum(grad_norm_one * normed_one, axis=0))
        grad_shift_one = lax.optimization_barrier(jnp.sum(grad_norm_one, axis=0))
        grad_in = grad_mixed + norm_back(grad_norm_one, first_gain, normed_one, inverse_one)
        terms = (grad_gain_one, grad_shift_one, grad_qkv_w, grad_bias, grad_out_w, grad_gain_two, grad_shift_two, grad_gate_w, grad_up_w, grad_down)
        totals = tuple((total + term for total, term in zip(totals, terms)))
        return (totals, (output, grad_in))
    start = (jnp.zeros((D,), jnp.float32), jnp.zeros((D,), jnp.float32), jnp.zeros((D, 3 * D), jnp.float32), jnp.zeros((3 * D,), jnp.float32), jnp.zeros((D, D), jnp.float32), jnp.zeros((D,), jnp.float32), jnp.zeros((D,), jnp.float32), jnp.zeros((D, FF), jnp.float32), jnp.zeros((D, FF), jnp.float32), jnp.zeros((FF, D), jnp.float32))
    totals, stacked = lax.scan(one_group, start, (inputs_all, cot_all, pos_all, block_table))
    outputs = stacked[0].reshape(TOKENS, D)
    grad_inputs = stacked[1].reshape(TOKENS, D)
    return (outputs, grad_inputs, totals[0], totals[1], totals[2], totals[3], totals[4], totals[5], totals[6], totals[7], totals[8], totals[9])
```

```python
import jax
import jax.numpy as jnp
from jax import lax
from jax.sharding import PartitionSpec as P

HD = 64
ROT = 16
BLOCK = 128


EPS = 1e-05


def layer_norm(values, gain, shift):
    average = jnp.mean(values, axis=-1, keepdims=True)
    centred = values - average
    inverse = lax.rsqrt(jnp.mean(centred * centred, axis=-1, keepdims=True) + EPS)
    normed = centred * inverse
    return (normed * gain + shift, normed, inverse)


def norm_back(upstream, gain, normed, inverse):
    scaled = upstream * gain
    centred = scaled - jnp.mean(scaled, axis=-1, keepdims=True)
    return inverse * (centred - normed * jnp.mean(scaled * normed, axis=-1, keepdims=True))


def rotary_tables(token_pos):
    half_rot = ROT // 2
    freqs = 10000.0 ** (-2.0 * jnp.arange(half_rot, dtype=jnp.float32) / ROT)
    angles = token_pos.astype(jnp.float32)[:, None] * freqs[None, :]
    return (jnp.cos(angles)[:, None, :], jnp.sin(angles)[:, None, :])


def rotate(field, cosine, sine):
    half_rot = ROT // 2
    first = field[..., :half_rot]
    second = field[..., half_rot:ROT]
    return jnp.concatenate(
        [first * cosine - second * sine, second * cosine + first * sine, field[..., ROT:]], axis=-1
    )


def logical_index(table_row):
    offsets = jnp.tile(jnp.arange(BLOCK, dtype=jnp.int32), table_row.shape[0])
    return jnp.repeat(table_row, BLOCK) * BLOCK + offsets


def attend(query_rot, key_rot, value_b, visible, scale):
    scores = (
        jnp.einsum("qhd,khd->hqk", query_rot, key_rot, preferred_element_type=jnp.float32) * scale
    )
    log_total = jnp.log(jnp.sum(jnp.where(visible, jnp.exp(scores), 0.0), axis=-1))
    prob_b = jnp.where(visible, jnp.exp(scores - log_total[..., None]), 0.0).astype(jnp.bfloat16)
    attended = jnp.einsum(
        "hqk,khd->qhd", prob_b, value_b, preferred_element_type=jnp.float32
    ).astype(jnp.bfloat16)
    return (attended, log_total)


def attend_back(query_rot, key_rot, value_b, visible, scale, log_total, attended, grad_att):
    scores = (
        jnp.einsum("qhd,khd->hqk", query_rot, key_rot, preferred_element_type=jnp.float32) * scale
    )
    prob = jnp.where(visible, jnp.exp(scores - log_total[..., None]), 0.0)
    prob_back = prob.astype(jnp.bfloat16)
    grad_value = jnp.einsum("hqk,qhd->khd", prob_back, grad_att, preferred_element_type=jnp.float32)
    grad_prob = jnp.einsum("qhd,khd->hqk", grad_att, value_b, preferred_element_type=jnp.float32)
    delta = jnp.sum(grad_att.astype(jnp.float32) * attended.astype(jnp.float32), axis=-1).T
    grad_scores = (prob * (grad_prob - delta[..., None]) * scale).astype(jnp.bfloat16)
    grad_query = jnp.einsum(
        "hqk,khd->qhd", grad_scores, key_rot, preferred_element_type=jnp.float32
    )
    grad_key = jnp.einsum(
        "hqk,qhd->khd", grad_scores, query_rot, preferred_element_type=jnp.float32
    )
    return (grad_query, grad_key, grad_value)


def xor_pairs(size, mask):
    return [(i, i ^ mask) for i in range(size)]


def swap(value, axis, mask):
    return lax.ppermute(value, axis, xor_pairs(lax.axis_size(axis), mask))


def ctx_exchange(parts):
    size, rows, cols = parts.shape
    here = lax.axis_index("ctx")
    own = lax.dynamic_index_in_dim(parts, here, 0, keepdims=False)
    result = jnp.zeros((size * rows, cols), parts.dtype)
    result = lax.dynamic_update_slice(result, own, (here * rows, 0))
    for mask in range(1, size):
        there = here ^ mask
        got = swap(lax.dynamic_index_in_dim(parts, there, 0, keepdims=False), "ctx", mask)
        result = lax.dynamic_update_slice(result, got, (there * rows, 0))
    return result


def ctx_gather(rows_own):
    size = lax.axis_size("ctx")
    rows, cols = rows_own.shape
    here = lax.axis_index("ctx")
    result = jnp.zeros((size * rows, cols), rows_own.dtype)
    result = lax.dynamic_update_slice(result, rows_own, (here * rows, 0))
    for mask in range(1, size):
        got = swap(rows_own, "ctx", mask)
        result = lax.dynamic_update_slice(result, got, ((here ^ mask) * rows, 0))
    return result


def dp_gather(block):
    size = lax.axis_size("dp")
    here = lax.axis_index("dp")
    rows, cols = block.shape
    half = rows // 2 // 8 * 8
    got = {0: block}
    for mask in range(2, size, 2):
        if mask & (mask - 1) == 0:
            got[mask] = swap(block, "dp", mask)
    for mask in range(2, size, 2):
        if mask & (mask - 1):
            low = mask & -mask
            high = mask ^ low
            if high & (high - 1) == 0:
                got[mask] = jnp.concatenate(
                    [swap(got[low][:half], "dp", high), swap(got[high][half:], "dp", low)], axis=0
                )
            else:
                got[mask] = swap(block, "dp", mask)
    for mask in range(0, size, 2):
        got[mask | 1] = swap(got[mask], "dp", 1)
    result = jnp.zeros((size * rows, cols), block.dtype)
    for mask in range(size):
        result = lax.dynamic_update_slice(result, got[mask], ((here ^ mask) * rows, 0))
    return result


def dp_scatter(partial):
    size = lax.axis_size("dp")
    here = lax.axis_index("dp")
    total, cols = partial.shape
    rows = total // size

    def block(mask):
        return lax.dynamic_slice(partial, ((here ^ mask) * rows, 0), (rows, cols))

    summed = {}
    for mask in range(0, size, 2):
        other = swap(block(mask | 1).astype(jnp.bfloat16), "dp", 1)
        summed[mask] = block(mask).astype(jnp.float32) + other.astype(jnp.float32)
    result = summed[0]
    for mask in range(2, size, 2):
        result = result + swap(summed[mask].astype(jnp.bfloat16), "dp", mask).astype(jnp.float32)
    return result


def ctx_return(block):
    size = lax.axis_size("ctx")
    here = lax.axis_index("ctx")
    rows = block.shape[0] // size
    cols = block.shape[1]
    narrow = block.astype(jnp.bfloat16)
    result = jnp.zeros((size, rows, cols), jnp.bfloat16)
    own = lax.dynamic_slice(narrow, (here * rows, 0), (rows, cols))
    result = lax.dynamic_update_slice(result, own[None], (here, 0, 0))
    for mask in range(1, size):
        there = here ^ mask
        got = swap(lax.dynamic_slice(narrow, (there * rows, 0), (rows, cols)), "ctx", mask)
        result = lax.dynamic_update_slice(result, got[None], (there, 0, 0))
    return result.astype(jnp.float32)


def sum_rows(partial_value):
    return lax.psum_scatter(
        partial_value.astype(jnp.bfloat16), "ctx", scatter_dimension=0, tiled=True
    ).astype(jnp.float32)


def shards(
    layer_input,
    block_table,
    positions,
    first_gain,
    first_shift,
    qkv_weight,
    qkv_bias,
    out_weight,
    second_gain,
    second_shift,
    gate_weight,
    up_weight,
    down_weight,
    cotangent,
):
    count, width = layer_input.shape
    scale = HD ** (-0.5)
    parts = lax.axis_size("ctx")
    groups_dp = lax.axis_size("dp")
    ctx_index = lax.axis_index("ctx")
    dp_index = lax.axis_index("dp")
    quarter = width // parts
    local_heads = quarter // HD
    hidden = gate_weight.shape[1]
    units = hidden // (groups_dp * parts)
    local_units = hidden // parts
    rows_here = first_gain.shape[0]
    bias_here = qkv_bias.shape[0]

    qkv_parts = qkv_weight.reshape(rows_here, 3, parts, quarter).transpose(2, 0, 1, 3)
    qkv_parts = qkv_parts.reshape(parts, rows_here, 3 * quarter)
    gate_parts = gate_weight.reshape(rows_here, groups_dp, parts, units).transpose(2, 0, 1, 3)
    up_parts = up_weight.reshape(rows_here, groups_dp, parts, units).transpose(2, 0, 1, 3)
    pair_parts = jnp.concatenate(
        [
            gate_parts.reshape(parts, rows_here, local_units),
            up_parts.reshape(parts, rows_here, local_units),
        ],
        axis=2,
    )
    proj_cols = dp_gather(ctx_exchange(qkv_parts))
    out_full = dp_gather(ctx_gather(out_weight))
    pair_cols = dp_gather(ctx_exchange(pair_parts))
    down_part = dp_gather(down_weight)

    small = jnp.concatenate(
        [
            first_gain,
            first_shift,
            second_gain,
            second_shift,
            qkv_bias,
            positions.astype(jnp.float32),
        ]
    )
    small_all = lax.all_gather(small, ("dp", "ctx"), axis=0, tiled=False)
    gain_one = small_all[:, :rows_here].reshape(width)
    shift_one = small_all[:, rows_here : 2 * rows_here].reshape(width)
    gain_two = small_all[:, 2 * rows_here : 3 * rows_here].reshape(width)
    shift_two = small_all[:, 3 * rows_here : 4 * rows_here].reshape(width)
    bias_full = small_all[:, 4 * rows_here : 4 * rows_here + bias_here].reshape(3, parts, quarter)
    bias_three = lax.dynamic_index_in_dim(bias_full, ctx_index, axis=1, keepdims=False)
    pos_all = small_all[:, 4 * rows_here + bias_here :].reshape(groups_dp, parts * count)
    group_pos = lax.dynamic_index_in_dim(pos_all, dp_index, axis=0, keepdims=False).astype(jnp.int32)

    group_input = lax.all_gather(layer_input, "ctx", axis=0, tiled=True)
    group_cot = lax.all_gather(cotangent, "ctx", axis=0, tiled=True)
    group_count = group_input.shape[0]
    own_start = ctx_index * count
    key_index = logical_index(block_table[0])
    visible = (key_index[None, :] <= key_index[:, None]) & (
        key_index[None, :] >= key_index[:, None] - group_pos[:, None]
    )
    visible = visible[None]
    cosine, sine = rotary_tables(group_pos)

    inputs = group_input.astype(jnp.float32)
    norm_one, normed_one, inverse_one = layer_norm(inputs, gain_one, shift_one)
    norm_one_b = norm_one.astype(jnp.bfloat16)
    proj = jnp.dot(norm_one_b, proj_cols, preferred_element_type=jnp.float32)
    query = proj[:, :quarter] + bias_three[0]
    keyproj = proj[:, quarter : 2 * quarter] + bias_three[1]
    value = proj[:, 2 * quarter :] + bias_three[2]
    query_rot = rotate(query.reshape(group_count, local_heads, HD), cosine, sine).astype(
        jnp.bfloat16
    )
    key_rot = rotate(keyproj.reshape(group_count, local_heads, HD), cosine, sine).astype(
        jnp.bfloat16
    )
    value_b = value.reshape(group_count, local_heads, HD).astype(jnp.bfloat16)
    attended, log_total = attend(query_rot, key_rot, value_b, visible, scale)
    heads_full = lax.all_gather(attended.reshape(group_count, quarter), "ctx", axis=1, tiled=True)
    mixed = inputs + jnp.dot(heads_full, out_full, preferred_element_type=jnp.float32)
    norm_two, normed_two, inverse_two = layer_norm(mixed, gain_two, shift_two)
    norm_two_b = norm_two.astype(jnp.bfloat16)
    pair = jnp.dot(norm_two_b, pair_cols, preferred_element_type=jnp.float32)
    gate = pair[:, :local_units]
    upval = pair[:, local_units:]
    sigma = jax.nn.sigmoid(gate)
    act_b = (gate * sigma * upval).astype(jnp.bfloat16)
    feed_out = sum_rows(jnp.dot(act_b, down_part, preferred_element_type=jnp.float32))
    mixed_own = lax.dynamic_slice_in_dim(mixed, own_start, count, 0)
    layer_output = (mixed_own + feed_out).astype(jnp.bfloat16)

    grad_down = jnp.dot(act_b.T, group_cot, preferred_element_type=jnp.float32)
    grad_act = jnp.dot(group_cot, down_part.T, preferred_element_type=jnp.float32)
    grad_gate_b = (grad_act * upval * sigma * (1.0 + gate * (1.0 - sigma))).astype(jnp.bfloat16)
    grad_up_b = (grad_act * gate * sigma).astype(jnp.bfloat16)
    grad_pair_b = jnp.concatenate([grad_gate_b, grad_up_b], axis=1)
    norm_two_part = jnp.dot(grad_pair_b, pair_cols.T, preferred_element_type=jnp.float32)
    grad_two_own = sum_rows(norm_two_part)
    grad_gain_two = jnp.sum(norm_two_part * normed_two, axis=0)
    grad_shift_two = jnp.sum(norm_two_part, axis=0)
    grad_pair_w = jnp.dot(norm_two_b.T, grad_pair_b, preferred_element_type=jnp.float32)
    normed_two_own = lax.dynamic_slice_in_dim(normed_two, own_start, count, 0)
    inverse_two_own = lax.dynamic_slice_in_dim(inverse_two, own_start, count, 0)
    grad_mixed_own = cotangent.astype(jnp.float32) + norm_back(
        grad_two_own, gain_two, normed_two_own, inverse_two_own
    )
    grad_mixed_b = lax.all_gather(
        grad_mixed_own.astype(jnp.bfloat16), "ctx", axis=0, tiled=True
    )
    out_rows = lax.dynamic_slice_in_dim(out_full, ctx_index * quarter, quarter, 0)
    grad_att = jnp.dot(grad_mixed_b, out_rows.T, preferred_element_type=jnp.float32)
    grad_att = grad_att.astype(jnp.bfloat16).reshape(group_count, local_heads, HD)
    mixed_grad_cols = lax.dynamic_slice_in_dim(grad_mixed_b, ctx_index * quarter, quarter, 1)
    grad_out_w = jnp.dot(heads_full.T, mixed_grad_cols, preferred_element_type=jnp.float32)
    grad_query, grad_key, grad_value = attend_back(
        query_rot, key_rot, value_b, visible, scale, log_total, attended, grad_att
    )
    grad_query = rotate(grad_query, cosine, -sine).reshape(group_count, quarter)
    grad_key = rotate(grad_key, cosine, -sine).reshape(group_count, quarter)
    grad_value = grad_value.reshape(group_count, quarter)
    bias_local = jnp.stack(
        [jnp.sum(grad_query, axis=0), jnp.sum(grad_key, axis=0), jnp.sum(grad_value, axis=0)]
    )
    bias_spread = lax.dynamic_update_slice_in_dim(
        jnp.zeros((3, parts, quarter), jnp.float32), bias_local[:, None, :], ctx_index, 1
    )
    grad_proj_b = jnp.concatenate([grad_query, grad_key, grad_value], axis=-1).astype(jnp.bfloat16)
    norm_one_part = jnp.dot(grad_proj_b, proj_cols.T, preferred_element_type=jnp.float32)
    grad_norm_one = sum_rows(norm_one_part)
    grad_gain_one = jnp.sum(norm_one_part * normed_one, axis=0)
    grad_shift_one = jnp.sum(norm_one_part, axis=0)
    grad_qkv_w = jnp.dot(norm_one_b.T, grad_proj_b, preferred_element_type=jnp.float32)
    normed_one_own = lax.dynamic_slice_in_dim(normed_one, own_start, count, 0)
    inverse_one_own = lax.dynamic_slice_in_dim(inverse_one, own_start, count, 0)
    grad_input = grad_mixed_own + norm_back(
        grad_norm_one, gain_one, normed_one_own, inverse_one_own
    )

    everyone = groups_dp * parts
    small_grads = jnp.concatenate(
        [
            grad_gain_one.reshape(everyone, rows_here),
            grad_shift_one.reshape(everyone, rows_here),
            grad_gain_two.reshape(everyone, rows_here),
            grad_shift_two.reshape(everyone, rows_here),
            bias_spread.reshape(everyone, bias_here),
        ],
        axis=1,
    )
    small_got = lax.all_to_all(small_grads, ("dp", "ctx"), split_axis=0, concat_axis=0, tiled=True)
    small_own = jnp.sum(small_got, axis=0)

    down_own = dp_scatter(grad_down)
    pair_own = ctx_return(dp_scatter(grad_pair_w))
    out_own = ctx_return(dp_scatter(grad_out_w))
    qkv_own = ctx_return(dp_scatter(grad_qkv_w))
    pair_own = pair_own.reshape(parts, rows_here, 2, groups_dp, units)
    pair_own = pair_own.transpose(2, 1, 3, 0, 4).reshape(2, rows_here, hidden)
    out_own = out_own.transpose(1, 0, 2).reshape(rows_here, width)
    qkv_own = qkv_own.reshape(parts, rows_here, 3, quarter).transpose(1, 2, 0, 3)
    qkv_own = qkv_own.reshape(rows_here, 3 * width)
    return (
        layer_output,
        grad_input,
        small_own[:rows_here],
        small_own[rows_here : 2 * rows_here],
        qkv_own,
        small_own[4 * rows_here :],
        out_own,
        small_own[2 * rows_here : 3 * rows_here],
        small_own[3 * rows_here : 4 * rows_here],
        pair_own[0],
        pair_own[1],
        down_own,
    )


def solution(mesh):
    return jax.shard_map(
        shards,
        mesh=mesh,
        in_specs=(
            P(("dp", "ctx"), None),
            P("dp", None),
            P(("dp", "ctx")),
            P(("dp", "ctx")),
            P(("dp", "ctx")),
            P(("dp", "ctx"), None),
            P(("dp", "ctx")),
            P(("dp", "ctx"), None),
            P(("dp", "ctx")),
            P(("dp", "ctx")),
            P(("dp", "ctx"), None),
            P(("dp", "ctx"), None),
            P(("dp", "ctx"), None),
            P(("dp", "ctx"), None),
        ),
        out_specs=(
            P(("dp", "ctx"), None),
            P(("dp", "ctx"), None),
            P(("dp", "ctx")),
            P(("dp", "ctx")),
            P(("dp", "ctx"), None),
            P(("dp", "ctx")),
            P(("dp", "ctx"), None),
            P(("dp", "ctx")),
            P(("dp", "ctx")),
            P(("dp", "ctx"), None),
            P(("dp", "ctx"), None),
            P(("dp", "ctx"), None),
        ),
        check_vma=False,
    )
```

```python
import jax
import jax.numpy as jnp
from jax import lax
from jax.experimental import pallas as pl
from jax.experimental.pallas import tpu as pltpu
from jax.sharding import PartitionSpec as P

HD = 64
ROT = 16
BLOCK = 128


EPS = 1e-05


def layer_norm(values, gain, shift):
    average = jnp.mean(values, axis=-1, keepdims=True)
    centred = values - average
    inverse = lax.rsqrt(jnp.mean(centred * centred, axis=-1, keepdims=True) + EPS)
    normed = centred * inverse
    return (normed * gain + shift, normed, inverse)


def norm_back(upstream, gain, normed, inverse):
    scaled = upstream * gain
    centred = scaled - jnp.mean(scaled, axis=-1, keepdims=True)
    return inverse * (centred - normed * jnp.mean(scaled * normed, axis=-1, keepdims=True))


def rotary_tables(token_pos):
    half_rot = ROT // 2
    freqs = 10000.0 ** (-2.0 * jnp.arange(half_rot, dtype=jnp.float32) / ROT)
    angles = token_pos.astype(jnp.float32)[:, None] * freqs[None, :]
    return (jnp.cos(angles)[:, None, :], jnp.sin(angles)[:, None, :])


def rotate(field, cosine, sine):
    half_rot = ROT // 2
    first = field[..., :half_rot]
    second = field[..., half_rot:ROT]
    return jnp.concatenate(
        [first * cosine - second * sine, second * cosine + first * sine, field[..., ROT:]], axis=-1
    )


def logical_index(table_row):
    offsets = jnp.tile(jnp.arange(BLOCK, dtype=jnp.int32), table_row.shape[0])
    return jnp.repeat(table_row, BLOCK) * BLOCK + offsets


def attend(query_rot, key_rot, value_b, visible, scale):
    scores = (
        jnp.einsum("qhd,khd->hqk", query_rot, key_rot, preferred_element_type=jnp.float32) * scale
    )
    log_total = jnp.log(jnp.sum(jnp.where(visible, jnp.exp(scores), 0.0), axis=-1))
    prob_b = jnp.where(visible, jnp.exp(scores - log_total[..., None]), 0.0).astype(jnp.bfloat16)
    attended = jnp.einsum(
        "hqk,khd->qhd", prob_b, value_b, preferred_element_type=jnp.float32
    ).astype(jnp.bfloat16)
    return (attended, log_total)


def attend_back(query_rot, key_rot, value_b, visible, scale, log_total, attended, grad_att):
    scores = (
        jnp.einsum("qhd,khd->hqk", query_rot, key_rot, preferred_element_type=jnp.float32) * scale
    )
    prob = jnp.where(visible, jnp.exp(scores - log_total[..., None]), 0.0)
    prob_back = prob.astype(jnp.bfloat16)
    grad_value = jnp.einsum("hqk,qhd->khd", prob_back, grad_att, preferred_element_type=jnp.float32)
    grad_prob = jnp.einsum("qhd,khd->hqk", grad_att, value_b, preferred_element_type=jnp.float32)
    delta = jnp.sum(grad_att.astype(jnp.float32) * attended.astype(jnp.float32), axis=-1).T
    grad_scores = (prob * (grad_prob - delta[..., None]) * scale).astype(jnp.bfloat16)
    grad_query = jnp.einsum(
        "hqk,khd->qhd", grad_scores, key_rot, preferred_element_type=jnp.float32
    )
    grad_key = jnp.einsum(
        "hqk,qhd->khd", grad_scores, query_rot, preferred_element_type=jnp.float32
    )
    return (grad_query, grad_key, grad_value)

LANES = 128
VMEM_BYTES = 56 * 1024 * 1024


def after(value, *deps):
    return lax.optimization_barrier((value, deps))[0]


def swap(value, axis, mask):
    return lax.ppermute(value, axis, [(i, i ^ mask) for i in range(lax.axis_size(axis))])


def place(pieces, here):
    rows, cols = pieces[0].shape
    result = jnp.zeros((len(pieces) * rows, cols), pieces[0].dtype)
    for mask, piece in enumerate(pieces):
        result = lax.dynamic_update_slice(result, piece, ((here ^ mask) * rows, 0))
    return result


def ctx_exchange(parts):
    here = lax.axis_index("ctx")
    picked = [
        lax.dynamic_index_in_dim(parts, here ^ mask, 0, keepdims=False)
        for mask in range(parts.shape[0])
    ]
    return picked[:1] + [swap(picked[mask], "ctx", mask) for mask in range(1, len(picked))]


def ctx_gather(rows_own):
    return [rows_own] + [
        swap(rows_own, "ctx", mask) for mask in range(1, lax.axis_size("ctx"))
    ]


def one_bit(mask):
    return mask & (mask - 1) == 0


def gather_first(block):
    size = lax.axis_size("dp")
    got = {0: block}
    for mask in range(2, size, 2):
        if one_bit(mask):
            got[mask] = swap(block, "dp", mask)
    return got


def gather_second(got):
    size = lax.axis_size("dp")
    got = dict(got)
    rows = got[0].shape[0]
    half = rows // 16 * 8
    for mask in range(2, size, 2):
        if one_bit(mask):
            continue
        low = mask & -mask
        high = mask ^ low
        if one_bit(high):
            got[mask] = (
                swap(got[low][:half], "dp", high),
                swap(got[high][half:], "dp", low),
            )
        else:
            got[mask] = swap(got[0], "dp", mask)
    return got


def gather_last(got):
    size = lax.axis_size("dp")
    pieces = []
    for mask in range(0, size, 2):
        mine = got[mask]
        if isinstance(mine, tuple):
            theirs = tuple(swap(piece, "dp", 1) for piece in mine)
            pieces.append(jnp.concatenate(mine, axis=0))
            pieces.append(jnp.concatenate(theirs, axis=0))
        else:
            pieces.append(mine)
            pieces.append(swap(mine, "dp", 1))
    return pieces


def ready(pieces, here):
    if pieces[0].shape[0] % LANES == 0:
        return pieces, here
    return [place(pieces, here)], jnp.zeros_like(here)


def tile_of(cols, most):
    best = LANES
    for tile in range(LANES, most + 1, LANES):
        if cols % tile == 0:
            best = tile
    return best


def matmul_pieces(x, pieces, here, added, most):
    count = x.shape[0]
    total = len(pieces)
    rows, cols = pieces[0].shape
    tile = tile_of(cols, most)

    def kernel(index, x_ref, added_ref, *refs):
        out = refs[total]
        acc = added_ref[...].astype(jnp.float32)
        for mask in range(total):
            start = pl.multiple_of((index[0] ^ mask) * rows, LANES)
            acc = acc + jnp.dot(
                x_ref[:, pl.ds(start, rows)], refs[mask][...], preferred_element_type=jnp.float32
            )
        out[...] = acc

    return pl.pallas_call(
        kernel,
        out_shape=jax.ShapeDtypeStruct((count, cols), jnp.float32),
        grid_spec=pltpu.PrefetchScalarGridSpec(
            num_scalar_prefetch=1,
            grid=(cols // tile,),
            in_specs=[
                pl.BlockSpec(x.shape, lambda i, s: (0, 0)),
                pl.BlockSpec((added.shape[0], tile), lambda i, s: (0, i)),
            ]
            + [pl.BlockSpec((rows, tile), lambda i, s: (0, i))] * total,
            out_specs=pl.BlockSpec((count, tile), lambda i, s: (0, i)),
        ),
        compiler_params=pltpu.CompilerParams(vmem_limit_bytes=VMEM_BYTES),
        name="matmul_pieces",
    )(here.reshape(1), x, added, *pieces)


def matmul_back(g, pieces, here):
    count, cols = g.shape
    total = len(pieces)
    rows = pieces[0].shape[0]

    def kernel(index, g_ref, *refs):
        out, buffer, sem = refs[total:]
        copies = [
            pltpu.make_async_copy(refs[mask], buffer.at[mask], sem.at[mask])
            for mask in range(total)
        ]
        for copy in copies:
            copy.start()
        for mask in range(total):
            copies[mask].wait()
            part = lax.dot_general(
                g_ref[...],
                buffer[mask],
                (((1,), (1,)), ((), ())),
                preferred_element_type=jnp.float32,
            )
            start = pl.multiple_of((index[0] ^ mask) * rows, LANES)
            out[:, pl.ds(start, rows)] = part.astype(jnp.bfloat16)

    return pl.pallas_call(
        kernel,
        out_shape=jax.ShapeDtypeStruct((count, total * rows), jnp.bfloat16),
        grid_spec=pltpu.PrefetchScalarGridSpec(
            num_scalar_prefetch=1,
            grid=(1,),
            in_specs=[pl.BlockSpec(g.shape, lambda i, s: (0, 0))]
            + [pl.BlockSpec(memory_space=pl.ANY)] * total,
            out_specs=pl.BlockSpec((count, total * rows), lambda i, s: (0, 0)),
            scratch_shapes=[
                pltpu.VMEM((total, rows, cols), jnp.bfloat16),
                pltpu.SemaphoreType.DMA((total,)),
            ],
        ),
        compiler_params=pltpu.CompilerParams(vmem_limit_bytes=VMEM_BYTES),
        name="matmul_back",
    )(here.reshape(1), g, *pieces)


def feed_forward(norm_b, cot, pieces, here, down):
    count, width = cot.shape
    total = len(pieces)
    rows, cols = pieces[0].shape
    units = cols // 2
    tile = 2 * LANES

    def kernel(index, x_ref, cot_ref, down_ref, *refs):
        act_ref, grad_ref = refs[total:]
        pair = None
        for mask in range(total):
            start = pl.multiple_of((index[0] ^ mask) * rows, LANES)
            part = jnp.dot(
                x_ref[:, pl.ds(start, rows)], refs[mask][...], preferred_element_type=jnp.float32
            )
            pair = part if pair is None else pair + part
        grad_act = lax.dot_general(
            cot_ref[...],
            down_ref[...],
            (((1,), (1,)), ((), ())),
            preferred_element_type=jnp.float32,
        )
        for k in range(tile // LANES):
            gate = pair[:, 2 * k * LANES : (2 * k + 1) * LANES]
            upval = pair[:, (2 * k + 1) * LANES : (2 * k + 2) * LANES]
            upstream = grad_act[:, k * LANES : (k + 1) * LANES]
            sigma = 1.0 / (1.0 + jnp.exp(-gate))
            silu = gate * sigma
            act_ref[:, k * LANES : (k + 1) * LANES] = (silu * upval).astype(jnp.bfloat16)
            grad_ref[:, 2 * k * LANES : (2 * k + 1) * LANES] = (
                upstream * upval * sigma * (1.0 + gate * (1.0 - sigma))
            ).astype(jnp.bfloat16)
            grad_ref[:, (2 * k + 1) * LANES : (2 * k + 2) * LANES] = (upstream * silu).astype(
                jnp.bfloat16
            )

    return pl.pallas_call(
        kernel,
        out_shape=(
            jax.ShapeDtypeStruct((count, units), jnp.bfloat16),
            jax.ShapeDtypeStruct((count, cols), jnp.bfloat16),
        ),
        grid_spec=pltpu.PrefetchScalarGridSpec(
            num_scalar_prefetch=1,
            grid=(pl.cdiv(units, tile),),
            in_specs=[
                pl.BlockSpec(norm_b.shape, lambda i, s: (0, 0)),
                pl.BlockSpec(cot.shape, lambda i, s: (0, 0)),
                pl.BlockSpec((tile, width), lambda i, s: (i, 0)),
            ]
            + [pl.BlockSpec((rows, 2 * tile), lambda i, s: (0, i))] * total,
            out_specs=(
                pl.BlockSpec((count, tile), lambda i, s: (0, i)),
                pl.BlockSpec((count, 2 * tile), lambda i, s: (0, i)),
            ),
        ),
        compiler_params=pltpu.CompilerParams(vmem_limit_bytes=VMEM_BYTES),
        name="feed_forward",
    )(here.reshape(1), norm_b, cot, down, *pieces)


def weight_blocks(x, g, odd):
    size = lax.axis_size("dp")
    here = lax.axis_index("dp")
    rows = x.shape[1] // size
    blocks = {}
    for mask in range(1 if odd else 0, size, 2):
        cut = lax.dynamic_slice_in_dim(x, (here ^ mask) * rows, rows, 1)
        blocks[mask] = lax.dot_general(
            cut, g, (((0,), (0,)), ((), ())), preferred_element_type=jnp.float32
        )
    return blocks


def row_blocks(partial, odd):
    size = lax.axis_size("dp")
    here = lax.axis_index("dp")
    rows = partial.shape[0] // size
    return {
        mask: lax.dynamic_slice_in_dim(partial, (here ^ mask) * rows, rows, 0)
        for mask in range(1 if odd else 0, size, 2)
    }


def to_partner(blocks):
    return {mask: swap(block.astype(jnp.bfloat16), "dp", 1) for mask, block in blocks.items()}


def with_partner(blocks, got):
    return {mask: block + got[mask | 1].astype(jnp.float32) for mask, block in blocks.items()}


def to_owners(blocks):
    return {
        mask: swap(block.astype(jnp.bfloat16), "dp", mask) if mask else block
        for mask, block in blocks.items()
    }


def total_of(got):
    result = got[0]
    for mask, block in got.items():
        if mask:
            result = result + block.astype(jnp.float32)
    return result


def ctx_return(block):
    size = lax.axis_size("ctx")
    here = lax.axis_index("ctx")
    rows = block.shape[0] // size
    narrow = block.astype(jnp.bfloat16)
    picked = [
        lax.dynamic_slice_in_dim(narrow, (here ^ mask) * rows, rows, 0) for mask in range(size)
    ]
    got = picked[:1] + [swap(picked[mask], "ctx", mask) for mask in range(1, size)]
    result = jnp.zeros((size,) + got[0].shape, jnp.bfloat16)
    for mask in range(size):
        result = lax.dynamic_update_slice(result, got[mask][None], (here ^ mask, 0, 0))
    return result.astype(jnp.float32)


def sum_rows(partial_value):
    return lax.psum_scatter(
        partial_value.astype(jnp.bfloat16), "ctx", scatter_dimension=0, tiled=True
    ).astype(jnp.float32)


def shards(
    layer_input,
    block_table,
    positions,
    first_gain,
    first_shift,
    qkv_weight,
    qkv_bias,
    out_weight,
    second_gain,
    second_shift,
    gate_weight,
    up_weight,
    down_weight,
    cotangent,
):
    count, width = layer_input.shape
    scale = HD ** (-0.5)
    parts = lax.axis_size("ctx")
    groups_dp = lax.axis_size("dp")
    ctx_index = lax.axis_index("ctx")
    dp_index = lax.axis_index("dp")
    quarter = width // parts
    local_heads = quarter // HD
    hidden = gate_weight.shape[1]
    units = hidden // (groups_dp * parts)
    local_units = hidden // parts
    unit_blocks = local_units // LANES
    rows_here = first_gain.shape[0]
    bias_here = qkv_bias.shape[0]
    everyone = groups_dp * parts

    qkv_parts = qkv_weight.reshape(rows_here, 3, parts, quarter).transpose(2, 0, 1, 3)
    qkv_parts = qkv_parts.reshape(parts, rows_here, 3 * quarter)
    qkv_block = place(ctx_exchange(qkv_parts), ctx_index)
    group_input = lax.all_gather(layer_input, "ctx", axis=0, tiled=True)

    small = jnp.concatenate(
        [
            first_gain,
            first_shift,
            second_gain,
            second_shift,
            qkv_bias,
            positions.astype(jnp.float32),
        ]
    )
    small_size = small.shape[0]
    small_rows = -(-small_size // (8 * LANES)) * 8
    small = jnp.pad(small, (0, small_rows * LANES - small_size)).reshape(small_rows, LANES)
    small = after(small, qkv_parts)
    small_all = lax.all_gather(small, "ctx", axis=0, tiled=True)
    small_all = lax.all_gather(small_all, "dp", axis=0, tiled=True)
    small_all = small_all.reshape(everyone, small_rows * LANES)
    gain_one = small_all[:, :rows_here].reshape(width)
    shift_one = small_all[:, rows_here : 2 * rows_here].reshape(width)
    gain_two = small_all[:, 2 * rows_here : 3 * rows_here].reshape(width)
    shift_two = small_all[:, 3 * rows_here : 4 * rows_here].reshape(width)
    bias_full = small_all[:, 4 * rows_here : 4 * rows_here + bias_here].reshape(3, parts, quarter)
    bias_three = lax.dynamic_index_in_dim(bias_full, ctx_index, axis=1, keepdims=False)
    pos_all = small_all[:, 4 * rows_here + bias_here : small_size]
    pos_all = pos_all.reshape(groups_dp, parts * count)
    group_pos = lax.dynamic_index_in_dim(pos_all, dp_index, axis=0, keepdims=False).astype(jnp.int32)

    qkv_got = gather_first(qkv_block)

    gate_parts = gate_weight.reshape(rows_here, groups_dp, parts, units).transpose(2, 0, 1, 3)
    up_parts = up_weight.reshape(rows_here, groups_dp, parts, units).transpose(2, 0, 1, 3)
    pair_parts = jnp.stack(
        [
            gate_parts.reshape(parts, rows_here, unit_blocks, LANES),
            up_parts.reshape(parts, rows_here, unit_blocks, LANES),
        ],
        axis=3,
    ).reshape(parts, rows_here, 2 * local_units)
    pair_parts, out_rows_own = after((pair_parts, out_weight), qkv_block)
    out_block = place(ctx_gather(out_rows_own), ctx_index)
    pair_block = place(ctx_exchange(pair_parts), ctx_index)

    qkv_got = gather_second(qkv_got)
    second_done = [piece for mask, piece in qkv_got.items() if mask and not one_bit(mask)]
    out_block, pair_block = after((out_block, pair_block), *second_done)
    out_got = gather_first(out_block)
    pair_got = gather_first(pair_block)
    qkv_pieces, qkv_here = ready(gather_last(qkv_got), dp_index)

    group_cot = lax.all_gather(cotangent, "ctx", axis=0, tiled=True)
    group_count = group_input.shape[0]
    own_start = ctx_index * count
    key_index = logical_index(block_table[0])
    visible = (key_index[None, :] <= key_index[:, None]) & (
        key_index[None, :] >= key_index[:, None] - group_pos[:, None]
    )
    visible = visible[None]
    cosine, sine = rotary_tables(group_pos)

    inputs = group_input.astype(jnp.float32)
    norm_one, normed_one, inverse_one = layer_norm(inputs, gain_one, shift_one)
    norm_one_b = norm_one.astype(jnp.bfloat16)
    norm_one_b = after(norm_one_b, out_block, pair_block)
    proj = matmul_pieces(norm_one_b, qkv_pieces, qkv_here, bias_three.reshape(1, 3 * quarter), 512)
    query = proj[:, :quarter]
    keyproj = proj[:, quarter : 2 * quarter]
    value = proj[:, 2 * quarter :]
    query_rot = rotate(query.reshape(group_count, local_heads, HD), cosine, sine).astype(
        jnp.bfloat16
    )
    key_rot = rotate(keyproj.reshape(group_count, local_heads, HD), cosine, sine).astype(
        jnp.bfloat16
    )
    value_b = value.reshape(group_count, local_heads, HD).astype(jnp.bfloat16)
    attended, log_total = attend(query_rot, key_rot, value_b, visible, scale)
    attended_flat = attended.reshape(group_count, quarter)
    heads_full = lax.all_gather(attended_flat, "ctx", axis=1, tiled=True)

    out_got, pair_got = after((out_got, pair_got), attended_flat)
    out_got = gather_second(out_got)
    pair_got = gather_second(pair_got)
    down_block = after(down_weight, out_got[max(m for m in out_got if one_bit(m))])
    down_got = gather_second(gather_first(down_block))
    out_pieces_all = gather_last(out_got)
    pair_pieces_all = gather_last(pair_got)
    out_pieces, out_here = ready(out_pieces_all, dp_index)
    pair_pieces, pair_here = ready(pair_pieces_all, dp_index)
    down_part = place(gather_last(down_got), dp_index)

    mixed = matmul_pieces(heads_full, out_pieces, out_here, group_input, 512)
    norm_two, _, _ = layer_norm(mixed, gain_two, shift_two)
    norm_two_b = norm_two.astype(jnp.bfloat16)
    mixed_own = lax.dynamic_slice_in_dim(mixed, own_start, count, 0)
    _, normed_two_own, inverse_two_own = layer_norm(mixed_own, gain_two, shift_two)
    act_b, grad_pair_b = feed_forward(norm_two_b, group_cot, pair_pieces, pair_here, down_part)
    norm_two_part = matmul_back(grad_pair_b, pair_pieces, pair_here)
    grad_two_own = sum_rows(norm_two_part)

    norm_two_late, act_late, grad_pair_late = after(
        (norm_two_b, act_b, grad_pair_b), norm_two_part
    )
    pair_sent = to_partner(weight_blocks(norm_two_late, grad_pair_late, True))
    grad_down = lax.dot_general(
        act_late, group_cot, (((0,), (0,)), ((), ())), preferred_element_type=jnp.float32
    )
    down_sent = to_partner(row_blocks(grad_down, True))
    feed_part = jnp.dot(act_late, down_part, preferred_element_type=jnp.float32).astype(
        jnp.bfloat16
    )
    pair_sums = with_partner(weight_blocks(norm_two_late, grad_pair_late, False), pair_sent)
    down_sums = with_partner(row_blocks(grad_down, False), down_sent)
    pair_way = to_owners(pair_sums)
    down_way = to_owners(down_sums)

    grad_two_own = after(grad_two_own, feed_part, pair_sums)
    grad_gain_two = jnp.sum(grad_two_own * normed_two_own, axis=0)
    grad_shift_two = jnp.sum(grad_two_own, axis=0)
    grad_mixed_own = cotangent.astype(jnp.float32) + norm_back(
        grad_two_own, gain_two, normed_two_own, inverse_two_own
    )
    grad_mixed_own_b = grad_mixed_own.astype(jnp.bfloat16)
    grad_mixed_b = lax.all_gather(grad_mixed_own_b, "ctx", axis=0, tiled=True)
    feed_out = sum_rows(after(feed_part, grad_mixed_own_b))
    layer_output = (mixed_own + feed_out).astype(jnp.bfloat16)

    out_full = place(out_pieces_all, dp_index) if len(out_pieces) > 1 else out_pieces[0]
    out_rows = lax.dynamic_slice_in_dim(out_full, ctx_index * quarter, quarter, 0)
    grad_att = lax.dot_general(
        grad_mixed_b, out_rows, (((1,), (1,)), ((), ())), preferred_element_type=jnp.float32
    )
    grad_att = grad_att.astype(jnp.bfloat16).reshape(group_count, local_heads, HD)
    grad_query, grad_key, grad_value = attend_back(
        query_rot, key_rot, value_b, visible, scale, log_total, attended, grad_att
    )
    grad_query = rotate(grad_query, cosine, -sine).reshape(group_count, quarter)
    grad_key = rotate(grad_key, cosine, -sine).reshape(group_count, quarter)
    grad_value = grad_value.reshape(group_count, quarter)
    bias_local = jnp.stack(
        [jnp.sum(grad_query, axis=0), jnp.sum(grad_key, axis=0), jnp.sum(grad_value, axis=0)]
    )
    bias_spread = lax.dynamic_update_slice_in_dim(
        jnp.zeros((3, parts, quarter), jnp.float32), bias_local[:, None, :], ctx_index, 1
    )
    grad_proj_b = jnp.concatenate([grad_query, grad_key, grad_value], axis=-1).astype(jnp.bfloat16)
    norm_one_part = matmul_back(grad_proj_b, qkv_pieces, qkv_here)
    grad_norm_one = sum_rows(norm_one_part)

    norm_one_late, grad_proj_late = after((norm_one_b, grad_proj_b), norm_one_part)
    qkv_sent = to_partner(weight_blocks(norm_one_late, grad_proj_late, True))
    mixed_grad_cols = lax.dynamic_slice_in_dim(grad_mixed_b, ctx_index * quarter, quarter, 1)
    mixed_grad_cols = after(mixed_grad_cols, norm_one_part)
    out_sent = to_partner(weight_blocks(heads_full, mixed_grad_cols, True))
    qkv_sums = with_partner(weight_blocks(norm_one_late, grad_proj_late, False), qkv_sent)
    qkv_way = to_owners(qkv_sums)
    out_sums = with_partner(weight_blocks(heads_full, mixed_grad_cols, False), out_sent)
    out_way = to_owners(out_sums)

    pair_way, down_way = after((pair_way, down_way), norm_one_part)
    pair_own = ctx_return(total_of(pair_way))
    down_own = total_of(down_way)

    normed_one_late = after(normed_one, norm_one_part)
    part_f32 = norm_one_part.astype(jnp.float32)
    grad_gain_one = jnp.sum(part_f32 * normed_one_late, axis=0)
    grad_shift_one = jnp.sum(part_f32, axis=0)
    small_grads = jnp.concatenate(
        [
            grad_gain_one.reshape(everyone, rows_here),
            grad_shift_one.reshape(everyone, rows_here),
            grad_gain_two.reshape(everyone, rows_here),
            grad_shift_two.reshape(everyone, rows_here),
            bias_spread.reshape(everyone, bias_here),
        ],
        axis=1,
    )
    small_got = lax.all_to_all(small_grads, ("dp", "ctx"), split_axis=0, concat_axis=0, tiled=True)
    small_own = jnp.sum(small_got, axis=0)

    qkv_own = ctx_return(total_of(qkv_way))
    out_own = ctx_return(total_of(out_way))
    normed_one_own = lax.dynamic_slice_in_dim(normed_one, own_start, count, 0)
    inverse_one_own = lax.dynamic_slice_in_dim(inverse_one, own_start, count, 0)
    grad_input = grad_mixed_own + norm_back(
        grad_norm_one, gain_one, normed_one_own, inverse_one_own
    )

    pair_own = pair_own.reshape(parts, rows_here, unit_blocks, 2, LANES)
    pair_own = pair_own.transpose(3, 1, 0, 2, 4).reshape(2, rows_here, parts, groups_dp, units)
    pair_own = pair_own.transpose(0, 1, 3, 2, 4).reshape(2, rows_here, hidden)
    out_own = out_own.transpose(1, 0, 2).reshape(rows_here, width)
    qkv_own = qkv_own.reshape(parts, rows_here, 3, quarter).transpose(1, 2, 0, 3)
    qkv_own = qkv_own.reshape(rows_here, 3 * width)
    return (
        layer_output,
        grad_input,
        small_own[:rows_here],
        small_own[rows_here : 2 * rows_here],
        qkv_own,
        small_own[4 * rows_here :],
        out_own,
        small_own[2 * rows_here : 3 * rows_here],
        small_own[3 * rows_here : 4 * rows_here],
        pair_own[0],
        pair_own[1],
        down_own,
    )


def solution(mesh):
    return jax.shard_map(
        shards,
        mesh=mesh,
        in_specs=(
            P(("dp", "ctx"), None),
            P("dp", None),
            P(("dp", "ctx")),
            P(("dp", "ctx")),
            P(("dp", "ctx")),
            P(("dp", "ctx"), None),
            P(("dp", "ctx")),
            P(("dp", "ctx"), None),
            P(("dp", "ctx")),
            P(("dp", "ctx")),
            P(("dp", "ctx"), None),
            P(("dp", "ctx"), None),
            P(("dp", "ctx"), None),
            P(("dp", "ctx"), None),
        ),
        out_specs=(
            P(("dp", "ctx"), None),
            P(("dp", "ctx"), None),
            P(("dp", "ctx")),
            P(("dp", "ctx")),
            P(("dp", "ctx"), None),
            P(("dp", "ctx")),
            P(("dp", "ctx"), None),
            P(("dp", "ctx")),
            P(("dp", "ctx")),
            P(("dp", "ctx"), None),
            P(("dp", "ctx"), None),
            P(("dp", "ctx"), None),
        ),
        check_vma=False,
    )
```

```python
import jax
import jax.numpy as jnp
from jax import lax
from jax.experimental import pallas as pl
from jax.experimental.pallas import tpu as pltpu
from jax.sharding import PartitionSpec as P

HD = 64
ROT = 16
BLOCK = 128


EPS = 1e-05


def layer_norm(values, gain, shift):
    average = jnp.mean(values, axis=-1, keepdims=True)
    centred = values - average
    inverse = lax.rsqrt(jnp.mean(centred * centred, axis=-1, keepdims=True) + EPS)
    normed = centred * inverse
    return (normed * gain + shift, normed, inverse)


def norm_back(upstream, gain, normed, inverse):
    scaled = upstream * gain
    centred = scaled - jnp.mean(scaled, axis=-1, keepdims=True)
    return inverse * (centred - normed * jnp.mean(scaled * normed, axis=-1, keepdims=True))


def rotary_tables(token_pos, copies):
    half_rot = ROT // 2
    freqs = 10000.0 ** (-2.0 * jnp.arange(half_rot, dtype=jnp.float32) / ROT)
    angles = token_pos.astype(jnp.float32)[:, None] * freqs[None, :]
    cosine = jnp.cos(angles)
    sine = jnp.sin(angles)
    rest = jnp.zeros((token_pos.shape[0], HD - ROT), jnp.float32)
    zero = jnp.zeros_like(sine)
    keep = jnp.concatenate([cosine, cosine, rest + 1.0], axis=1)
    down = jnp.concatenate([-sine, zero, rest], axis=1)
    up = jnp.concatenate([zero, sine, rest], axis=1)
    return tuple(jnp.concatenate([table] * copies, axis=1) for table in (keep, down, up))


def logical_index(table_row):
    offsets = jnp.tile(jnp.arange(BLOCK, dtype=jnp.int32), table_row.shape[0])
    return jnp.repeat(table_row, BLOCK) * BLOCK + offsets


LANES = 128
VMEM_BYTES = 56 * 1024 * 1024


def after(value, *deps):
    return lax.optimization_barrier((value, deps))[0]


def swap(value, axis, mask):
    return lax.ppermute(value, axis, [(i, i ^ mask) for i in range(lax.axis_size(axis))])


def whole_call(kernel, out_shapes, here, *args, scratch=()):
    return pl.pallas_call(
        kernel,
        out_shape=out_shapes,
        in_specs=[pl.BlockSpec(memory_space=pltpu.SMEM)]
        + [pl.BlockSpec(memory_space=pltpu.VMEM)] * len(args),
        out_specs=jax.tree.map(lambda _: pl.BlockSpec(memory_space=pltpu.VMEM), out_shapes),
        scratch_shapes=list(scratch),
        compiler_params=pltpu.CompilerParams(vmem_limit_bytes=VMEM_BYTES),
    )(here.reshape(1), *args)


def pick_columns(weight, fields, parts, here):
    rows, cols = weight.shape
    wide = cols // (fields * parts)

    def kernel(index, source, *outs):
        for mask in range(parts):
            part = index[0] ^ mask
            for field in range(fields):
                start = pl.multiple_of((field * parts + part) * wide, LANES)
                outs[mask][:, field * wide : (field + 1) * wide] = source[:, pl.ds(start, wide)]

    shape = jax.ShapeDtypeStruct((rows, fields * wide), weight.dtype)
    return list(whole_call(kernel, (shape,) * parts, here, weight))


def unpick_columns(pieces, fields, here):
    parts = len(pieces)
    rows, cols = pieces[0].shape
    wide = cols // fields

    def kernel(index, *refs):
        out = refs[parts]
        for mask in range(parts):
            part = index[0] ^ mask
            for field in range(fields):
                start = pl.multiple_of((field * parts + part) * wide, LANES)
                out[:, pl.ds(start, wide)] = refs[mask][
                    :, field * wide : (field + 1) * wide
                ].astype(jnp.float32)

    shape = jax.ShapeDtypeStruct((rows, parts * cols), jnp.float32)
    return whole_call(kernel, shape, here, *pieces)


def pick_units(gate, up, groups, parts, here):
    rows, hidden = gate.shape
    units = hidden // (groups * parts)
    local = hidden // parts

    def kernel(index, gate_ref, up_ref, *refs):
        outs, scratch = refs[:parts], refs[parts]
        for side, ref in enumerate((gate_ref, up_ref)):
            value = ref[...]
            for part in range(parts):
                mine = jnp.concatenate(
                    [
                        value[:, (g * parts + part) * units : (g * parts + part + 1) * units]
                        for g in range(groups)
                    ],
                    axis=1,
                )
                for k in range(local // LANES):
                    at = (2 * k + side) * LANES
                    scratch[part, :, at : at + LANES] = mine[:, k * LANES : (k + 1) * LANES]
        for mask in range(parts):
            outs[mask][...] = scratch[index[0] ^ mask]

    shape = jax.ShapeDtypeStruct((rows, 2 * local), gate.dtype)
    return list(
        whole_call(
            kernel,
            (shape,) * parts,
            here,
            gate,
            up,
            scratch=[pltpu.VMEM((parts, rows, 2 * local), gate.dtype)],
        )
    )


def unpick_units(pieces, groups, here):
    parts = len(pieces)
    rows, cols = pieces[0].shape
    local = cols // 2
    units = local // groups

    def kernel(index, *refs):
        outs, scratch = refs[parts : parts + 2], refs[parts + 2]
        for mask in range(parts):
            scratch[index[0] ^ mask] = refs[mask][...].astype(jnp.float32)
        for side in range(2):
            mine = []
            for part in range(parts):
                mine.append(
                    jnp.concatenate(
                        [
                            scratch[part, :, (2 * k + side) * LANES : (2 * k + side + 1) * LANES]
                            for k in range(local // LANES)
                        ],
                        axis=1,
                    )
                )
            outs[side][...] = jnp.concatenate(
                [
                    mine[part][:, g * units : (g + 1) * units]
                    for g in range(groups)
                    for part in range(parts)
                ],
                axis=1,
            )

    shape = jax.ShapeDtypeStruct((rows, local * parts), jnp.float32)
    return whole_call(
        kernel,
        (shape, shape),
        here,
        *pieces,
        scratch=[pltpu.VMEM((parts, rows, cols), jnp.float32)],
    )


def stack_rows(pieces, here):
    parts = len(pieces)
    rows, cols = pieces[0].shape

    def kernel(index, *refs):
        for mask in range(parts):
            start = pl.multiple_of((index[0] ^ mask) * rows, 16)
            refs[parts][pl.ds(start, rows), :] = refs[mask][...]

    shape = jax.ShapeDtypeStruct((parts * rows, cols), pieces[0].dtype)
    return whole_call(kernel, shape, here, *pieces)


def sum_and_pick(blocks, parts, here):
    total = len(blocks)
    rows, cols = blocks[0].shape
    rows = rows // parts

    def kernel(index, *refs):
        for mask in range(parts):
            start = pl.multiple_of((index[0] ^ mask) * rows, 16)
            value = refs[0][pl.ds(start, rows), :].astype(jnp.float32)
            for k in range(1, total):
                value = value + refs[k][pl.ds(start, rows), :].astype(jnp.float32)
            refs[total + mask][...] = value.astype(jnp.bfloat16)

    shape = jax.ShapeDtypeStruct((rows, cols), jnp.bfloat16)
    return list(whole_call(kernel, (shape,) * parts, here, *blocks))


def rotated(field, tables):
    half_rot = ROT // 2
    keep, down, up = tables
    lanes = field.shape[1]
    return (
        field * keep
        + pltpu.roll(field, lanes - half_rot, 1) * down
        + pltpu.roll(field, half_rot, 1) * up
    )


def mask_of(own_ref, low_ref, key_ref):
    return (key_ref[...] <= own_ref[...]) & (key_ref[...] >= low_ref[...])


def probabilities(query, key, visible):
    scores = lax.dot_general(
        query, key, (((1,), (1,)), ((), ())), preferred_element_type=jnp.float32
    ) * HD ** (-0.5)
    total = jnp.sum(jnp.where(visible, jnp.exp(scores), 0.0), axis=1, keepdims=True)
    return jnp.where(visible, jnp.exp(scores - jnp.log(total)), 0.0)


def attend(proj, tables, own_index, low_index, key_index):
    count, cols = proj.shape
    quarter = cols // 3
    steps = quarter // LANES

    def kernel(q_ref, k_ref, v_ref, c_ref, s_ref, t_ref, own, low, keys, qo, ko, vo, att):
        tables_here = (c_ref[...], s_ref[...], t_ref[...])
        query = rotated(q_ref[...], tables_here).astype(jnp.bfloat16)
        key = rotated(k_ref[...], tables_here).astype(jnp.bfloat16)
        value = v_ref[...].astype(jnp.bfloat16)
        qo[...] = query
        ko[...] = key
        vo[...] = value
        visible = mask_of(own, low, keys)
        for h in range(LANES // HD):
            cut = slice(h * HD, (h + 1) * HD)
            prob_b = probabilities(query[:, cut], key[:, cut], visible).astype(jnp.bfloat16)
            att[:, cut] = jnp.dot(
                prob_b, value[:, cut], preferred_element_type=jnp.float32
            ).astype(jnp.bfloat16)

    tile = pl.BlockSpec((count, LANES), lambda i: (0, i))
    full = pl.BlockSpec((count, LANES), lambda i: (0, 0))
    column = pl.BlockSpec((count, 1), lambda i: (0, 0))
    shape = jax.ShapeDtypeStruct((count, quarter), jnp.bfloat16)
    return pl.pallas_call(
        kernel,
        out_shape=(shape,) * 4,
        grid=(steps,),
        in_specs=[
            tile,
            pl.BlockSpec((count, LANES), lambda i: (0, i + steps)),
            pl.BlockSpec((count, LANES), lambda i: (0, i + 2 * steps)),
            full,
            full,
            full,
            column,
            column,
            pl.BlockSpec((1, count), lambda i: (0, 0)),
        ],
        out_specs=(tile,) * 4,
        compiler_params=pltpu.CompilerParams(vmem_limit_bytes=VMEM_BYTES),
        name="attend",
    )(proj, proj, proj, *tables, own_index, low_index, key_index)


def attend_back(saved, grad_mixed_b, out_rows, tables, own_index, low_index, key_index):
    query_all, key_all, value_all, attended = saved
    count, quarter = query_all.shape
    width = grad_mixed_b.shape[1]
    steps = quarter // LANES

    def kernel(q_ref, k_ref, v_ref, a_ref, g_ref, w_ref, c_ref, s_ref, t_ref, own, low, keys, out, sums):
        step = pl.program_id(0)
        visible = mask_of(own, low, keys)
        back = (c_ref[...], -s_ref[...], -t_ref[...])
        grad_att = lax.dot_general(
            g_ref[...], w_ref[...], (((1,), (1,)), ((), ())), preferred_element_type=jnp.float32
        ).astype(jnp.bfloat16)
        products = grad_att.astype(jnp.float32) * a_ref[...].astype(jnp.float32)
        query = q_ref[...]
        key = k_ref[...]
        value = v_ref[...]
        grads = ([], [], [])
        for h in range(LANES // HD):
            cut = slice(h * HD, (h + 1) * HD)
            prob = probabilities(query[:, cut], key[:, cut], visible)
            grad_value = lax.dot_general(
                prob.astype(jnp.bfloat16),
                grad_att[:, cut],
                (((0,), (0,)), ((), ())),
                preferred_element_type=jnp.float32,
            )
            grad_prob = lax.dot_general(
                grad_att[:, cut],
                value[:, cut],
                (((1,), (1,)), ((), ())),
                preferred_element_type=jnp.float32,
            )
            delta = jnp.sum(products[:, cut], axis=1, keepdims=True)
            grad_scores = (prob * (grad_prob - delta) * HD ** (-0.5)).astype(jnp.bfloat16)
            grads[0].append(
                jnp.dot(grad_scores, key[:, cut], preferred_element_type=jnp.float32)
            )
            grads[1].append(
                lax.dot_general(
                    grad_scores,
                    query[:, cut],
                    (((0,), (0,)), ((), ())),
                    preferred_element_type=jnp.float32,
                )
            )
            grads[2].append(grad_value)
        for field in range(3):
            grad = jnp.concatenate(grads[field], axis=1)
            if field < 2:
                grad = rotated(grad, back)
            start = pl.multiple_of(field * quarter + step * LANES, LANES)
            out[:, pl.ds(start, LANES)] = grad.astype(jnp.bfloat16)
            sums[:, pl.ds(start, LANES)] = jnp.sum(grad, axis=0, keepdims=True)

    tile = pl.BlockSpec((count, LANES), lambda i: (0, i))
    full = pl.BlockSpec((count, LANES), lambda i: (0, 0))
    column = pl.BlockSpec((count, 1), lambda i: (0, 0))
    return pl.pallas_call(
        kernel,
        out_shape=(
            jax.ShapeDtypeStruct((count, 3 * quarter), jnp.bfloat16),
            jax.ShapeDtypeStruct((1, 3 * quarter), jnp.float32),
        ),
        grid=(steps,),
        in_specs=[tile] * 4
        + [
            pl.BlockSpec((count, width), lambda i: (0, 0)),
            pl.BlockSpec((LANES, width), lambda i: (i, 0)),
            full,
            full,
            full,
            column,
            column,
            pl.BlockSpec((1, count), lambda i: (0, 0)),
        ],
        out_specs=(
            pl.BlockSpec((count, 3 * quarter), lambda i: (0, 0)),
            pl.BlockSpec((1, 3 * quarter), lambda i: (0, 0)),
        ),
        compiler_params=pltpu.CompilerParams(vmem_limit_bytes=VMEM_BYTES),
        name="attend_back",
    )(
        query_all,
        key_all,
        value_all,
        attended,
        grad_mixed_b,
        out_rows,
        *tables,
        own_index,
        low_index,
        key_index,
    )


def rows_of(pieces, here, part, wide):
    total = len(pieces)
    rows, cols = pieces[0].shape
    if total == 1:
        return lax.dynamic_slice_in_dim(pieces[0], part * wide, wide, 0)
    per = wide // rows

    def kernel(index, *refs):
        out, sem = refs[total], refs[total + 1]
        for mask in range(total):
            block = index[0] ^ mask

            @pl.when(block // per == index[1])
            def _(mask=mask, block=block):
                start = pl.multiple_of((block % per) * rows, 16)
                copy = pltpu.make_async_copy(refs[mask], out.at[pl.ds(start, rows), :], sem)
                copy.start()
                copy.wait()

    return pl.pallas_call(
        kernel,
        out_shape=jax.ShapeDtypeStruct((wide, cols), pieces[0].dtype),
        in_specs=[pl.BlockSpec(memory_space=pltpu.SMEM)]
        + [pl.BlockSpec(memory_space=pl.ANY)] * total,
        out_specs=pl.BlockSpec(memory_space=pltpu.VMEM),
        scratch_shapes=[pltpu.SemaphoreType.DMA],
        compiler_params=pltpu.CompilerParams(vmem_limit_bytes=VMEM_BYTES),
        name="rows_of",
    )(jnp.stack([here, part]), *pieces)


def place(pieces, here):
    rows, cols = pieces[0].shape
    result = jnp.zeros((len(pieces) * rows, cols), pieces[0].dtype)
    for mask, piece in enumerate(pieces):
        result = lax.dynamic_update_slice(result, piece, ((here ^ mask) * rows, 0))
    return result


def ctx_exchange(picked):
    return picked[:1] + [swap(picked[mask], "ctx", mask) for mask in range(1, len(picked))]


def ctx_gather(rows_own):
    return [rows_own] + [
        swap(rows_own, "ctx", mask) for mask in range(1, lax.axis_size("ctx"))
    ]


def one_bit(mask):
    return mask & (mask - 1) == 0


def gather_first(block):
    size = lax.axis_size("dp")
    got = {0: block}
    for mask in range(2, size, 2):
        if one_bit(mask):
            got[mask] = swap(block, "dp", mask)
    return got


def gather_second(got):
    size = lax.axis_size("dp")
    got = dict(got)
    rows = got[0].shape[0]
    half = rows // 16 * 8
    for mask in range(2, size, 2):
        if one_bit(mask):
            continue
        low = mask & -mask
        high = mask ^ low
        if one_bit(high):
            got[mask] = (
                swap(got[low][:half], "dp", high),
                swap(got[high][half:], "dp", low),
            )
        else:
            got[mask] = swap(got[0], "dp", mask)
    return got


def gather_last(got):
    size = lax.axis_size("dp")
    pieces = []
    for mask in range(0, size, 2):
        mine = got[mask]
        if isinstance(mine, tuple):
            theirs = tuple(swap(piece, "dp", 1) for piece in mine)
            pieces.append(jnp.concatenate(mine, axis=0))
            pieces.append(jnp.concatenate(theirs, axis=0))
        else:
            pieces.append(mine)
            pieces.append(swap(mine, "dp", 1))
    return pieces


def ready(pieces, here):
    if pieces[0].shape[0] % LANES == 0:
        return pieces, here
    return [place(pieces, here)], jnp.zeros_like(here)


def tile_of(cols, most):
    best = LANES
    for tile in range(LANES, most + 1, LANES):
        if cols % tile == 0:
            best = tile
    return best


def matmul_pieces(x, pieces, here, added, most):
    count = x.shape[0]
    total = len(pieces)
    rows, cols = pieces[0].shape
    tile = tile_of(cols, most)

    def kernel(index, x_ref, added_ref, *refs):
        out = refs[total]
        acc = added_ref[...].astype(jnp.float32)
        for mask in range(total):
            start = pl.multiple_of((index[0] ^ mask) * rows, LANES)
            acc = acc + jnp.dot(
                x_ref[:, pl.ds(start, rows)], refs[mask][...], preferred_element_type=jnp.float32
            )
        out[...] = acc

    return pl.pallas_call(
        kernel,
        out_shape=jax.ShapeDtypeStruct((count, cols), jnp.float32),
        grid_spec=pltpu.PrefetchScalarGridSpec(
            num_scalar_prefetch=1,
            grid=(cols // tile,),
            in_specs=[
                pl.BlockSpec(x.shape, lambda i, s: (0, 0)),
                pl.BlockSpec((added.shape[0], tile), lambda i, s: (0, i)),
            ]
            + [pl.BlockSpec((rows, tile), lambda i, s: (0, i))] * total,
            out_specs=pl.BlockSpec((count, tile), lambda i, s: (0, i)),
        ),
        compiler_params=pltpu.CompilerParams(vmem_limit_bytes=VMEM_BYTES),
        name="matmul_pieces",
    )(here.reshape(1), x, added, *pieces)


def matmul_back(g, pieces, here):
    count, cols = g.shape
    total = len(pieces)
    rows = pieces[0].shape[0]

    def kernel(index, g_ref, *refs):
        out, buffer, sem = refs[total:]
        copies = [
            pltpu.make_async_copy(refs[mask], buffer.at[mask], sem.at[mask])
            for mask in range(total)
        ]
        for copy in copies:
            copy.start()
        for mask in range(total):
            copies[mask].wait()
            part = lax.dot_general(
                g_ref[...],
                buffer[mask],
                (((1,), (1,)), ((), ())),
                preferred_element_type=jnp.float32,
            )
            start = pl.multiple_of((index[0] ^ mask) * rows, LANES)
            out[:, pl.ds(start, rows)] = part.astype(jnp.bfloat16)

    return pl.pallas_call(
        kernel,
        out_shape=jax.ShapeDtypeStruct((count, total * rows), jnp.bfloat16),
        grid_spec=pltpu.PrefetchScalarGridSpec(
            num_scalar_prefetch=1,
            grid=(1,),
            in_specs=[pl.BlockSpec(g.shape, lambda i, s: (0, 0))]
            + [pl.BlockSpec(memory_space=pl.ANY)] * total,
            out_specs=pl.BlockSpec((count, total * rows), lambda i, s: (0, 0)),
            scratch_shapes=[
                pltpu.VMEM((total, rows, cols), jnp.bfloat16),
                pltpu.SemaphoreType.DMA((total,)),
            ],
        ),
        compiler_params=pltpu.CompilerParams(vmem_limit_bytes=VMEM_BYTES),
        name="matmul_back",
    )(here.reshape(1), g, *pieces)


def feed_forward(norm_b, cot, pieces, here, down):
    count, width = cot.shape
    total = len(pieces)
    rows, cols = pieces[0].shape
    units = cols // 2
    tile = 2 * LANES

    def kernel(index, x_ref, cot_ref, down_ref, *refs):
        act_ref, grad_ref = refs[total:]
        pair = None
        for mask in range(total):
            start = pl.multiple_of((index[0] ^ mask) * rows, LANES)
            part = jnp.dot(
                x_ref[:, pl.ds(start, rows)], refs[mask][...], preferred_element_type=jnp.float32
            )
            pair = part if pair is None else pair + part
        grad_act = lax.dot_general(
            cot_ref[...],
            down_ref[...],
            (((1,), (1,)), ((), ())),
            preferred_element_type=jnp.float32,
        )
        for k in range(tile // LANES):
            gate = pair[:, 2 * k * LANES : (2 * k + 1) * LANES]
            upval = pair[:, (2 * k + 1) * LANES : (2 * k + 2) * LANES]
            upstream = grad_act[:, k * LANES : (k + 1) * LANES]
            sigma = 1.0 / (1.0 + jnp.exp(-gate))
            silu = gate * sigma
            act_ref[:, k * LANES : (k + 1) * LANES] = (silu * upval).astype(jnp.bfloat16)
            grad_ref[:, 2 * k * LANES : (2 * k + 1) * LANES] = (
                upstream * upval * sigma * (1.0 + gate * (1.0 - sigma))
            ).astype(jnp.bfloat16)
            grad_ref[:, (2 * k + 1) * LANES : (2 * k + 2) * LANES] = (upstream * silu).astype(
                jnp.bfloat16
            )

    return pl.pallas_call(
        kernel,
        out_shape=(
            jax.ShapeDtypeStruct((count, units), jnp.bfloat16),
            jax.ShapeDtypeStruct((count, cols), jnp.bfloat16),
        ),
        grid_spec=pltpu.PrefetchScalarGridSpec(
            num_scalar_prefetch=1,
            grid=(pl.cdiv(units, tile),),
            in_specs=[
                pl.BlockSpec(norm_b.shape, lambda i, s: (0, 0)),
                pl.BlockSpec(cot.shape, lambda i, s: (0, 0)),
                pl.BlockSpec((tile, width), lambda i, s: (i, 0)),
            ]
            + [pl.BlockSpec((rows, 2 * tile), lambda i, s: (0, i))] * total,
            out_specs=(
                pl.BlockSpec((count, tile), lambda i, s: (0, i)),
                pl.BlockSpec((count, 2 * tile), lambda i, s: (0, i)),
            ),
        ),
        compiler_params=pltpu.CompilerParams(vmem_limit_bytes=VMEM_BYTES),
        name="feed_forward",
    )(here.reshape(1), norm_b, cot, down, *pieces)


def weight_blocks(x, g, odd):
    size = lax.axis_size("dp")
    here = lax.axis_index("dp")
    rows = x.shape[1] // size
    blocks = {}
    for mask in range(1 if odd else 0, size, 2):
        cut = lax.dynamic_slice_in_dim(x, (here ^ mask) * rows, rows, 1)
        blocks[mask] = lax.dot_general(
            cut, g, (((0,), (0,)), ((), ())), preferred_element_type=jnp.float32
        )
    return blocks


def row_blocks(partial, odd):
    size = lax.axis_size("dp")
    here = lax.axis_index("dp")
    rows = partial.shape[0] // size
    return {
        mask: lax.dynamic_slice_in_dim(partial, (here ^ mask) * rows, rows, 0)
        for mask in range(1 if odd else 0, size, 2)
    }


def to_partner(blocks):
    return {mask: swap(block.astype(jnp.bfloat16), "dp", 1) for mask, block in blocks.items()}


def with_partner(blocks, got):
    return {mask: block + got[mask | 1].astype(jnp.float32) for mask, block in blocks.items()}


def to_owners(blocks):
    return {
        mask: swap(block.astype(jnp.bfloat16), "dp", mask) if mask else block
        for mask, block in blocks.items()
    }


def total_of(got):
    result = got[0]
    for mask, block in got.items():
        if mask:
            result = result + block.astype(jnp.float32)
    return result


def sum_rows(partial_value):
    return lax.psum_scatter(
        partial_value.astype(jnp.bfloat16), "ctx", scatter_dimension=0, tiled=True
    ).astype(jnp.float32)


def shards(
    layer_input,
    block_table,
    positions,
    first_gain,
    first_shift,
    qkv_weight,
    qkv_bias,
    out_weight,
    second_gain,
    second_shift,
    gate_weight,
    up_weight,
    down_weight,
    cotangent,
):
    count, width = layer_input.shape
    parts = lax.axis_size("ctx")
    groups_dp = lax.axis_size("dp")
    ctx_index = lax.axis_index("ctx")
    dp_index = lax.axis_index("dp")
    quarter = width // parts
    rows_here = first_gain.shape[0]
    bias_here = qkv_bias.shape[0]
    everyone = groups_dp * parts

    small = jnp.concatenate(
        [
            first_gain,
            first_shift,
            second_gain,
            second_shift,
            qkv_bias,
            positions.astype(jnp.float32),
        ]
    )
    small_size = small.shape[0]
    small_rows = -(-small_size // (8 * LANES)) * 8
    small = jnp.pad(small, (0, small_rows * LANES - small_size)).reshape(small_rows, LANES)
    small_line = lax.all_gather(small, "ctx", axis=0, tiled=True)

    qkv_first, layer_input = after((qkv_weight, layer_input), small_line)
    qkv_picked = pick_columns(qkv_first, 3, parts, ctx_index)
    qkv_line = ctx_exchange(qkv_picked)
    group_input = lax.all_gather(layer_input, "ctx", axis=0, tiled=True)

    small_all = lax.all_gather(after(small_line, qkv_picked), "dp", axis=0, tiled=True)
    small_all = small_all.reshape(everyone, small_rows * LANES)
    gain_one = small_all[:, :rows_here].reshape(width)
    shift_one = small_all[:, rows_here : 2 * rows_here].reshape(width)
    gain_two = small_all[:, 2 * rows_here : 3 * rows_here].reshape(width)
    shift_two = small_all[:, 3 * rows_here : 4 * rows_here].reshape(width)
    bias_full = small_all[:, 4 * rows_here : 4 * rows_here + bias_here]
    bias_full = bias_full.reshape(3, parts, quarter)
    bias_three = lax.dynamic_index_in_dim(bias_full, ctx_index, axis=1, keepdims=False)
    pos_all = small_all[:, 4 * rows_here + bias_here : small_size]
    pos_all = pos_all.reshape(groups_dp, parts * count)
    group_pos = lax.dynamic_index_in_dim(pos_all, dp_index, axis=0, keepdims=False)
    group_pos = group_pos.astype(jnp.int32)
    key_index = logical_index(block_table[0])
    low_index = (key_index - group_pos)[:, None]
    own_index = key_index[:, None]
    key_index = key_index[None, :]
    tables = rotary_tables(group_pos, LANES // HD)
    pair_picked = pick_units(gate_weight, up_weight, groups_dp, parts, ctx_index)

    qkv_block = stack_rows(qkv_line, ctx_index)
    qkv_got = gather_first(qkv_block)

    pair_picked, out_rows_own = after((pair_picked, out_weight), qkv_block)
    out_line = ctx_gather(out_rows_own)
    pair_line = ctx_exchange(pair_picked)

    qkv_got = gather_second(qkv_got)
    second_done = [piece for mask, piece in qkv_got.items() if mask and not one_bit(mask)]
    down_got = gather_first(after(down_weight, *second_done))
    qkv_pieces, qkv_here = ready(gather_last(qkv_got), dp_index)

    own_start = ctx_index * count
    inputs = group_input.astype(jnp.float32)
    norm_one, normed_one, inverse_one = layer_norm(inputs, gain_one, shift_one)
    norm_one_b = norm_one.astype(jnp.bfloat16)
    proj = matmul_pieces(norm_one_b, qkv_pieces, qkv_here, bias_three.reshape(1, 3 * quarter), 512)
    saved = attend(proj, tables, own_index, low_index, key_index)
    attended = saved[3]
    heads_full = lax.all_gather(attended, "ctx", axis=1, tiled=True)
    group_cot = lax.all_gather(after(cotangent, attended), "ctx", axis=0, tiled=True)

    out_line, pair_line, down_got = after((out_line, pair_line, down_got), attended)
    out_block = stack_rows(out_line, ctx_index)
    out_got = gather_first(out_block)
    down_got = gather_second(down_got)
    pair_line = after(pair_line, out_block)
    pair_block = stack_rows(pair_line, ctx_index)
    pair_got = gather_first(pair_block)
    down_pieces = gather_last(after(down_got, pair_block))
    down_part = place(down_pieces, dp_index)
    out_got = gather_second(out_got)
    pair_got = gather_second(pair_got)
    out_pieces, out_here = ready(gather_last(out_got), dp_index)
    pair_pieces, pair_here = ready(gather_last(pair_got), dp_index)
    out_rows = rows_of(out_pieces, out_here, ctx_index, quarter)

    mixed = matmul_pieces(heads_full, out_pieces, out_here, group_input, 512)
    norm_two, _, _ = layer_norm(mixed, gain_two, shift_two)
    norm_two_b = norm_two.astype(jnp.bfloat16)
    act_b, grad_pair_b = feed_forward(norm_two_b, group_cot, pair_pieces, pair_here, down_part)
    norm_two_part = matmul_back(grad_pair_b, pair_pieces, pair_here)
    grad_two_own = sum_rows(norm_two_part)

    norm_two_late, act_late, grad_pair_late, mixed_late = after(
        (norm_two_b, act_b, grad_pair_b, mixed), norm_two_part
    )
    pair_sent = to_partner(weight_blocks(norm_two_late, grad_pair_late, True))
    mixed_own = lax.dynamic_slice_in_dim(mixed_late, own_start, count, 0)
    _, normed_two_own, inverse_two_own = layer_norm(mixed_own, gain_two, shift_two)
    grad_down = lax.dot_general(
        act_late, group_cot, (((0,), (0,)), ((), ())), preferred_element_type=jnp.float32
    )
    down_sent = to_partner(row_blocks(grad_down, True))
    pair_sums = with_partner(weight_blocks(norm_two_late, grad_pair_late, False), pair_sent)
    pair_way = to_owners(pair_sums)
    act_late = after(act_late, pair_sums)
    feed_part = jnp.dot(act_late, down_part, preferred_element_type=jnp.float32).astype(
        jnp.bfloat16
    )
    down_sums = with_partner(row_blocks(grad_down, False), down_sent)
    down_way = to_owners(down_sums)

    grad_two_own = after(grad_two_own, feed_part, down_sums)
    grad_gain_two = jnp.sum(grad_two_own * normed_two_own, axis=0)
    grad_shift_two = jnp.sum(grad_two_own, axis=0)
    grad_mixed_own = cotangent.astype(jnp.float32) + norm_back(
        grad_two_own, gain_two, normed_two_own, inverse_two_own
    )
    grad_mixed_own_b = grad_mixed_own.astype(jnp.bfloat16)
    grad_mixed_b = lax.all_gather(grad_mixed_own_b, "ctx", axis=0, tiled=True)
    feed_out = sum_rows(after(feed_part, grad_mixed_own_b))

    grad_proj_b, bias_sums = attend_back(
        saved, grad_mixed_b, out_rows, tables, own_index, low_index, key_index
    )
    bias_spread = lax.dynamic_update_slice_in_dim(
        jnp.zeros((3, parts, quarter), jnp.float32),
        bias_sums.reshape(3, 1, quarter),
        ctx_index,
        1,
    )
    norm_one_part = matmul_back(grad_proj_b, qkv_pieces, qkv_here)
    grad_norm_one = sum_rows(norm_one_part)

    norm_one_late, grad_proj_late, grad_mixed_late = after(
        (norm_one_b, grad_proj_b, grad_mixed_b), norm_one_part
    )
    qkv_sent = to_partner(weight_blocks(norm_one_late, grad_proj_late, True))
    mixed_grad_cols = lax.dynamic_slice_in_dim(
        grad_mixed_late, ctx_index * quarter, quarter, 1
    )
    out_sent = to_partner(weight_blocks(heads_full, mixed_grad_cols, True))
    qkv_sums = with_partner(weight_blocks(norm_one_late, grad_proj_late, False), qkv_sent)
    qkv_way = to_owners(qkv_sums)
    mixed_grad_cols = after(mixed_grad_cols, qkv_sums)
    out_sums = with_partner(weight_blocks(heads_full, mixed_grad_cols, False), out_sent)
    out_way = to_owners(out_sums)

    pair_way, down_way = after((pair_way, down_way), out_sums)
    pair_cut = sum_and_pick(list(pair_way.values()), parts, ctx_index)
    pair_line_own = ctx_exchange(pair_cut)
    down_own = total_of(after(down_way, pair_cut))

    normed_one_late = after(normed_one, pair_cut)
    part_f32 = norm_one_part.astype(jnp.float32)
    grad_gain_one = jnp.sum(part_f32 * normed_one_late, axis=0)
    grad_shift_one = jnp.sum(part_f32, axis=0)
    small_grads = jnp.concatenate(
        [
            grad_gain_one.reshape(everyone, rows_here),
            grad_shift_one.reshape(everyone, rows_here),
            grad_gain_two.reshape(everyone, rows_here),
            grad_shift_two.reshape(everyone, rows_here),
            bias_spread.reshape(everyone, bias_here),
        ],
        axis=1,
    )
    small_got = lax.all_to_all(small_grads, ("dp", "ctx"), split_axis=0, concat_axis=0, tiled=True)
    small_own = jnp.sum(small_got, axis=0)

    qkv_way, out_way = after((qkv_way, out_way), pair_cut, down_own, small_grads)
    qkv_cut = sum_and_pick(list(qkv_way.values()), parts, ctx_index)
    qkv_line_own = ctx_exchange(qkv_cut)
    out_cut = sum_and_pick(list(after(out_way, qkv_cut).values()), parts, ctx_index)
    out_line_own = ctx_exchange(out_cut)
    gate_own, up_own = unpick_units(after(pair_line_own, out_cut), groups_dp, ctx_index)
    normed_one_own = lax.dynamic_slice_in_dim(normed_one, own_start, count, 0)
    inverse_one_own = lax.dynamic_slice_in_dim(inverse_one, own_start, count, 0)
    grad_norm_one = after(grad_norm_one, out_cut)
    grad_input = grad_mixed_own + norm_back(
        grad_norm_one, gain_one, normed_one_own, inverse_one_own
    )
    layer_output = (mixed_own + after(feed_out, norm_one_part)).astype(jnp.bfloat16)
    qkv_own = unpick_columns(qkv_line_own, 3, ctx_index)
    out_own = unpick_columns(out_line_own, 1, ctx_index)
    return (
        layer_output,
        grad_input,
        small_own[:rows_here],
        small_own[rows_here : 2 * rows_here],
        qkv_own,
        small_own[4 * rows_here :],
        out_own,
        small_own[2 * rows_here : 3 * rows_here],
        small_own[3 * rows_here : 4 * rows_here],
        gate_own,
        up_own,
        down_own,
    )


def solution(mesh):
    return jax.shard_map(
        shards,
        mesh=mesh,
        in_specs=(
            P(("dp", "ctx"), None),
            P("dp", None),
            P(("dp", "ctx")),
            P(("dp", "ctx")),
            P(("dp", "ctx")),
            P(("dp", "ctx"), None),
            P(("dp", "ctx")),
            P(("dp", "ctx"), None),
            P(("dp", "ctx")),
            P(("dp", "ctx")),
            P(("dp", "ctx"), None),
            P(("dp", "ctx"), None),
            P(("dp", "ctx"), None),
            P(("dp", "ctx"), None),
        ),
        out_specs=(
            P(("dp", "ctx"), None),
            P(("dp", "ctx"), None),
            P(("dp", "ctx")),
            P(("dp", "ctx")),
            P(("dp", "ctx"), None),
            P(("dp", "ctx")),
            P(("dp", "ctx"), None),
            P(("dp", "ctx")),
            P(("dp", "ctx")),
            P(("dp", "ctx"), None),
            P(("dp", "ctx"), None),
            P(("dp", "ctx"), None),
        ),
        check_vma=False,
    )
```

```python
import jax
import jax.numpy as jnp
from jax import lax
from jax.experimental import pallas as pl
from jax.experimental.pallas import tpu as pltpu
from jax.sharding import PartitionSpec as P

HD = 64
ROT = 16
BLOCK = 128


EPS = 1e-05


def layer_norm(values, gain, shift):
    average = jnp.mean(values, axis=-1, keepdims=True)
    centred = values - average
    inverse = lax.rsqrt(jnp.mean(centred * centred, axis=-1, keepdims=True) + EPS)
    normed = centred * inverse
    return (normed * gain + shift, normed, inverse)


def norm_back(upstream, gain, normed, inverse):
    scaled = upstream * gain
    centred = scaled - jnp.mean(scaled, axis=-1, keepdims=True)
    return inverse * (centred - normed * jnp.mean(scaled * normed, axis=-1, keepdims=True))


def rotary_tables(token_pos, copies):
    half_rot = ROT // 2
    freqs = 10000.0 ** (-2.0 * jnp.arange(half_rot, dtype=jnp.float32) / ROT)
    angles = token_pos.astype(jnp.float32)[:, None] * freqs[None, :]
    cosine = jnp.cos(angles)
    sine = jnp.sin(angles)
    rest = jnp.zeros((token_pos.shape[0], HD - ROT), jnp.float32)
    zero = jnp.zeros_like(sine)
    keep = jnp.concatenate([cosine, cosine, rest + 1.0], axis=1)
    down = jnp.concatenate([-sine, zero, rest], axis=1)
    up = jnp.concatenate([zero, sine, rest], axis=1)
    return tuple(jnp.concatenate([table] * copies, axis=1) for table in (keep, down, up))


def logical_index(table_row):
    offsets = jnp.tile(jnp.arange(BLOCK, dtype=jnp.int32), table_row.shape[0])
    return jnp.repeat(table_row, BLOCK) * BLOCK + offsets


LANES = 128
VMEM_BYTES = 56 * 1024 * 1024


def after(value, *deps):
    return lax.optimization_barrier((value, deps))[0]


def swap(value, axis, mask):
    return lax.ppermute(value, axis, [(i, i ^ mask) for i in range(lax.axis_size(axis))])


def whole_call(kernel, out_shapes, here, *args, scratch=()):
    return pl.pallas_call(
        kernel,
        out_shape=out_shapes,
        in_specs=[pl.BlockSpec(memory_space=pltpu.SMEM)]
        + [pl.BlockSpec(memory_space=pltpu.VMEM)] * len(args),
        out_specs=jax.tree.map(lambda _: pl.BlockSpec(memory_space=pltpu.VMEM), out_shapes),
        scratch_shapes=list(scratch),
        compiler_params=pltpu.CompilerParams(vmem_limit_bytes=VMEM_BYTES),
    )(here.reshape(1), *args)


def pick_columns(weight, fields, parts, here):
    rows, cols = weight.shape
    wide = cols // (fields * parts)

    def kernel(index, source, *outs):
        for mask in range(parts):
            part = index[0] ^ mask
            for field in range(fields):
                start = pl.multiple_of((field * parts + part) * wide, LANES)
                outs[mask][:, field * wide : (field + 1) * wide] = source[:, pl.ds(start, wide)]

    shape = jax.ShapeDtypeStruct((rows, fields * wide), weight.dtype)
    return list(whole_call(kernel, (shape,) * parts, here, weight))


def unpick_columns(pieces, fields, here):
    parts = len(pieces)
    rows, cols = pieces[0].shape
    wide = cols // fields

    def kernel(index, *refs):
        out = refs[parts]
        for mask in range(parts):
            part = index[0] ^ mask
            for field in range(fields):
                start = pl.multiple_of((field * parts + part) * wide, LANES)
                out[:, pl.ds(start, wide)] = refs[mask][
                    :, field * wide : (field + 1) * wide
                ].astype(jnp.float32)

    shape = jax.ShapeDtypeStruct((rows, parts * cols), jnp.float32)
    return whole_call(kernel, shape, here, *pieces)


def pick_units(gate, up, groups, parts, here):
    rows, hidden = gate.shape
    units = hidden // (groups * parts)
    local = hidden // parts

    def kernel(index, gate_ref, up_ref, *refs):
        outs, scratch = refs[:parts], refs[parts]
        for side, ref in enumerate((gate_ref, up_ref)):
            value = ref[...]
            for part in range(parts):
                mine = jnp.concatenate(
                    [
                        value[:, (g * parts + part) * units : (g * parts + part + 1) * units]
                        for g in range(groups)
                    ],
                    axis=1,
                )
                for k in range(local // LANES):
                    at = (2 * k + side) * LANES
                    scratch[part, :, at : at + LANES] = mine[:, k * LANES : (k + 1) * LANES]
        for mask in range(parts):
            outs[mask][...] = scratch[index[0] ^ mask]

    shape = jax.ShapeDtypeStruct((rows, 2 * local), gate.dtype)
    return list(
        whole_call(
            kernel,
            (shape,) * parts,
            here,
            gate,
            up,
            scratch=[pltpu.VMEM((parts, rows, 2 * local), gate.dtype)],
        )
    )


def unpick_units(pieces, groups, here):
    parts = len(pieces)
    rows, cols = pieces[0].shape
    local = cols // 2
    units = local // groups

    def kernel(index, *refs):
        outs, scratch = refs[parts : parts + 2], refs[parts + 2]
        for mask in range(parts):
            scratch[index[0] ^ mask] = refs[mask][...].astype(jnp.float32)
        for side in range(2):
            mine = []
            for part in range(parts):
                mine.append(
                    jnp.concatenate(
                        [
                            scratch[part, :, (2 * k + side) * LANES : (2 * k + side + 1) * LANES]
                            for k in range(local // LANES)
                        ],
                        axis=1,
                    )
                )
            outs[side][...] = jnp.concatenate(
                [
                    mine[part][:, g * units : (g + 1) * units]
                    for g in range(groups)
                    for part in range(parts)
                ],
                axis=1,
            )

    shape = jax.ShapeDtypeStruct((rows, local * parts), jnp.float32)
    return whole_call(
        kernel,
        (shape, shape),
        here,
        *pieces,
        scratch=[pltpu.VMEM((parts, rows, cols), jnp.float32)],
    )


def stack_rows(pieces, here, aligned=16):
    parts = len(pieces)
    rows, cols = pieces[0].shape

    def kernel(index, *refs):
        for mask in range(parts):
            start = pl.multiple_of((index[0] ^ mask) * rows, aligned)
            refs[parts][pl.ds(start, rows), :] = refs[mask][...]

    shape = jax.ShapeDtypeStruct((parts * rows, cols), pieces[0].dtype)
    return whole_call(kernel, shape, here, *pieces)


def sum_and_pick(blocks, parts, here):
    total = len(blocks)
    rows, cols = blocks[0].shape
    rows = rows // parts

    def kernel(index, *refs):
        for mask in range(parts):
            start = pl.multiple_of((index[0] ^ mask) * rows, 16)
            value = refs[0][pl.ds(start, rows), :].astype(jnp.float32)
            for k in range(1, total):
                value = value + refs[k][pl.ds(start, rows), :].astype(jnp.float32)
            refs[total + mask][...] = value.astype(jnp.bfloat16)

    shape = jax.ShapeDtypeStruct((rows, cols), jnp.bfloat16)
    return list(whole_call(kernel, (shape,) * parts, here, *blocks))


def rotated(field, tables):
    half_rot = ROT // 2
    keep, down, up = tables
    lanes = field.shape[1]
    return (
        field * keep
        + pltpu.roll(field, lanes - half_rot, 1) * down
        + pltpu.roll(field, half_rot, 1) * up
    )


def mask_of(own_ref, low_ref, key_ref):
    return (key_ref[...] <= own_ref[...]) & (key_ref[...] >= low_ref[...])


def probabilities(query, key, visible):
    scores = lax.dot_general(
        query, key, (((1,), (1,)), ((), ())), preferred_element_type=jnp.float32
    ) * HD ** (-0.5)
    total = jnp.sum(jnp.where(visible, jnp.exp(scores), 0.0), axis=1, keepdims=True)
    return jnp.where(visible, jnp.exp(scores - jnp.log(total)), 0.0)


def attend(proj, tables, own_index, low_index, key_index):
    count, cols = proj.shape
    quarter = cols // 3
    steps = quarter // LANES

    def kernel(q_ref, k_ref, v_ref, c_ref, s_ref, t_ref, own, low, keys, qo, ko, vo, att):
        tables_here = (c_ref[...], s_ref[...], t_ref[...])
        query = rotated(q_ref[...], tables_here).astype(jnp.bfloat16)
        key = rotated(k_ref[...], tables_here).astype(jnp.bfloat16)
        value = v_ref[...].astype(jnp.bfloat16)
        qo[...] = query
        ko[...] = key
        vo[...] = value
        visible = mask_of(own, low, keys)
        for h in range(LANES // HD):
            cut = slice(h * HD, (h + 1) * HD)
            prob_b = probabilities(query[:, cut], key[:, cut], visible).astype(jnp.bfloat16)
            att[:, cut] = jnp.dot(
                prob_b, value[:, cut], preferred_element_type=jnp.float32
            ).astype(jnp.bfloat16)

    tile = pl.BlockSpec((count, LANES), lambda i: (0, i))
    full = pl.BlockSpec((count, LANES), lambda i: (0, 0))
    column = pl.BlockSpec((count, 1), lambda i: (0, 0))
    shape = jax.ShapeDtypeStruct((count, quarter), jnp.bfloat16)
    return pl.pallas_call(
        kernel,
        out_shape=(shape,) * 4,
        grid=(steps,),
        in_specs=[
            tile,
            pl.BlockSpec((count, LANES), lambda i: (0, i + steps)),
            pl.BlockSpec((count, LANES), lambda i: (0, i + 2 * steps)),
            full,
            full,
            full,
            column,
            column,
            pl.BlockSpec((1, count), lambda i: (0, 0)),
        ],
        out_specs=(tile,) * 4,
        compiler_params=pltpu.CompilerParams(vmem_limit_bytes=VMEM_BYTES),
        name="attend",
    )(proj, proj, proj, *tables, own_index, low_index, key_index)


def attend_back(saved, grad_mixed_b, out_rows, tables, own_index, low_index, key_index):
    query_all, key_all, value_all, attended = saved
    count, quarter = query_all.shape
    width = grad_mixed_b.shape[1]
    steps = quarter // LANES

    def kernel(q_ref, k_ref, v_ref, a_ref, g_ref, w_ref, c_ref, s_ref, t_ref, own, low, keys, out, sums):
        step = pl.program_id(0)
        visible = mask_of(own, low, keys)
        back = (c_ref[...], -s_ref[...], -t_ref[...])
        grad_att = lax.dot_general(
            g_ref[...], w_ref[...], (((1,), (1,)), ((), ())), preferred_element_type=jnp.float32
        ).astype(jnp.bfloat16)
        products = grad_att.astype(jnp.float32) * a_ref[...].astype(jnp.float32)
        query = q_ref[...]
        key = k_ref[...]
        value = v_ref[...]
        grads = ([], [], [])
        for h in range(LANES // HD):
            cut = slice(h * HD, (h + 1) * HD)
            prob = probabilities(query[:, cut], key[:, cut], visible)
            grad_value = lax.dot_general(
                prob.astype(jnp.bfloat16),
                grad_att[:, cut],
                (((0,), (0,)), ((), ())),
                preferred_element_type=jnp.float32,
            )
            grad_prob = lax.dot_general(
                grad_att[:, cut],
                value[:, cut],
                (((1,), (1,)), ((), ())),
                preferred_element_type=jnp.float32,
            )
            delta = jnp.sum(products[:, cut], axis=1, keepdims=True)
            grad_scores = (prob * (grad_prob - delta) * HD ** (-0.5)).astype(jnp.bfloat16)
            grads[0].append(
                jnp.dot(grad_scores, key[:, cut], preferred_element_type=jnp.float32)
            )
            grads[1].append(
                lax.dot_general(
                    grad_scores,
                    query[:, cut],
                    (((0,), (0,)), ((), ())),
                    preferred_element_type=jnp.float32,
                )
            )
            grads[2].append(grad_value)
        for field in range(3):
            grad = jnp.concatenate(grads[field], axis=1)
            if field < 2:
                grad = rotated(grad, back)
            start = pl.multiple_of(field * quarter + step * LANES, LANES)
            out[:, pl.ds(start, LANES)] = grad.astype(jnp.bfloat16)
            sums[:, pl.ds(start, LANES)] = jnp.sum(grad, axis=0, keepdims=True)

    tile = pl.BlockSpec((count, LANES), lambda i: (0, i))
    full = pl.BlockSpec((count, LANES), lambda i: (0, 0))
    column = pl.BlockSpec((count, 1), lambda i: (0, 0))
    return pl.pallas_call(
        kernel,
        out_shape=(
            jax.ShapeDtypeStruct((count, 3 * quarter), jnp.bfloat16),
            jax.ShapeDtypeStruct((1, 3 * quarter), jnp.float32),
        ),
        grid=(steps,),
        in_specs=[tile] * 4
        + [
            pl.BlockSpec((count, width), lambda i: (0, 0)),
            pl.BlockSpec((LANES, width), lambda i: (i, 0)),
            full,
            full,
            full,
            column,
            column,
            pl.BlockSpec((1, count), lambda i: (0, 0)),
        ],
        out_specs=(
            pl.BlockSpec((count, 3 * quarter), lambda i: (0, 0)),
            pl.BlockSpec((1, 3 * quarter), lambda i: (0, 0)),
        ),
        compiler_params=pltpu.CompilerParams(vmem_limit_bytes=VMEM_BYTES),
        name="attend_back",
    )(
        query_all,
        key_all,
        value_all,
        attended,
        grad_mixed_b,
        out_rows,
        *tables,
        own_index,
        low_index,
        key_index,
    )


def rows_of(pieces, here, part, wide):
    total = len(pieces)
    rows, cols = pieces[0].shape
    if total == 1:
        return lax.dynamic_slice_in_dim(pieces[0], part * wide, wide, 0)
    per = wide // rows

    def kernel(index, *refs):
        out, sem = refs[total], refs[total + 1]
        for mask in range(total):
            block = index[0] ^ mask

            @pl.when(block // per == index[1])
            def _(mask=mask, block=block):
                start = pl.multiple_of((block % per) * rows, 16)
                copy = pltpu.make_async_copy(refs[mask], out.at[pl.ds(start, rows), :], sem)
                copy.start()
                copy.wait()

    return pl.pallas_call(
        kernel,
        out_shape=jax.ShapeDtypeStruct((wide, cols), pieces[0].dtype),
        in_specs=[pl.BlockSpec(memory_space=pltpu.SMEM)]
        + [pl.BlockSpec(memory_space=pl.ANY)] * total,
        out_specs=pl.BlockSpec(memory_space=pltpu.VMEM),
        scratch_shapes=[pltpu.SemaphoreType.DMA],
        compiler_params=pltpu.CompilerParams(vmem_limit_bytes=VMEM_BYTES),
        name="rows_of",
    )(jnp.stack([here, part]), *pieces)


def place(pieces, here):
    rows, cols = pieces[0].shape
    result = jnp.zeros((len(pieces) * rows, cols), pieces[0].dtype)
    for mask, piece in enumerate(pieces):
        result = lax.dynamic_update_slice(result, piece, ((here ^ mask) * rows, 0))
    return result


def ctx_exchange(picked):
    return picked[:1] + [swap(picked[mask], "ctx", mask) for mask in range(1, len(picked))]


def ctx_gather(rows_own):
    return [rows_own] + [
        swap(rows_own, "ctx", mask) for mask in range(1, lax.axis_size("ctx"))
    ]


def one_bit(mask):
    return mask & (mask - 1) == 0


def gather_first(block):
    size = lax.axis_size("dp")
    got = {0: block}
    for mask in range(2, size, 2):
        if one_bit(mask):
            got[mask] = swap(block, "dp", mask)
    return got


def gather_second(got):
    size = lax.axis_size("dp")
    got = dict(got)
    rows = got[0].shape[0]
    half = rows // 16 * 8
    for mask in range(2, size, 2):
        if one_bit(mask):
            continue
        low = mask & -mask
        high = mask ^ low
        if one_bit(high):
            got[mask] = (
                swap(got[low][:half], "dp", high),
                swap(got[high][half:], "dp", low),
            )
        else:
            got[mask] = swap(got[0], "dp", mask)
    return got


def gather_last(got):
    size = lax.axis_size("dp")
    pieces = []
    for mask in range(0, size, 2):
        mine = got[mask]
        if isinstance(mine, tuple):
            theirs = tuple(swap(piece, "dp", 1) for piece in mine)
            pieces.append(jnp.concatenate(mine, axis=0))
            pieces.append(jnp.concatenate(theirs, axis=0))
        else:
            pieces.append(mine)
            pieces.append(swap(mine, "dp", 1))
    return pieces


def ready(pieces, here):
    if pieces[0].shape[0] % LANES == 0:
        return pieces, here
    return [place(pieces, here)], jnp.zeros_like(here)


def tile_of(cols, most):
    best = LANES
    for tile in range(LANES, most + 1, LANES):
        if cols % tile == 0:
            best = tile
    return best


def matmul_pieces(x, pieces, here, added, most):
    count = x.shape[0]
    total = len(pieces)
    rows, cols = pieces[0].shape
    tile = tile_of(cols, most)

    def kernel(index, x_ref, added_ref, *refs):
        out = refs[total]
        acc = added_ref[...].astype(jnp.float32)
        for mask in range(total):
            start = pl.multiple_of((index[0] ^ mask) * rows, LANES)
            acc = acc + jnp.dot(
                x_ref[:, pl.ds(start, rows)], refs[mask][...], preferred_element_type=jnp.float32
            )
        out[...] = acc

    return pl.pallas_call(
        kernel,
        out_shape=jax.ShapeDtypeStruct((count, cols), jnp.float32),
        grid_spec=pltpu.PrefetchScalarGridSpec(
            num_scalar_prefetch=1,
            grid=(cols // tile,),
            in_specs=[
                pl.BlockSpec(x.shape, lambda i, s: (0, 0)),
                pl.BlockSpec((added.shape[0], tile), lambda i, s: (0, i)),
            ]
            + [pl.BlockSpec((rows, tile), lambda i, s: (0, i))] * total,
            out_specs=pl.BlockSpec((count, tile), lambda i, s: (0, i)),
        ),
        compiler_params=pltpu.CompilerParams(vmem_limit_bytes=VMEM_BYTES),
        name="matmul_pieces",
    )(here.reshape(1), x, added, *pieces)


def matmul_back(g, pieces, here):
    count, cols = g.shape
    total = len(pieces)
    rows = pieces[0].shape[0]

    def kernel(index, g_ref, *refs):
        out, buffer, sem = refs[total:]
        copies = [
            pltpu.make_async_copy(refs[mask], buffer.at[mask], sem.at[mask])
            for mask in range(total)
        ]
        for copy in copies:
            copy.start()
        for mask in range(total):
            copies[mask].wait()
            part = lax.dot_general(
                g_ref[...],
                buffer[mask],
                (((1,), (1,)), ((), ())),
                preferred_element_type=jnp.float32,
            )
            start = pl.multiple_of((index[0] ^ mask) * rows, LANES)
            out[:, pl.ds(start, rows)] = part.astype(jnp.bfloat16)

    return pl.pallas_call(
        kernel,
        out_shape=jax.ShapeDtypeStruct((count, total * rows), jnp.bfloat16),
        grid_spec=pltpu.PrefetchScalarGridSpec(
            num_scalar_prefetch=1,
            grid=(1,),
            in_specs=[pl.BlockSpec(g.shape, lambda i, s: (0, 0))]
            + [pl.BlockSpec(memory_space=pl.ANY)] * total,
            out_specs=pl.BlockSpec((count, total * rows), lambda i, s: (0, 0)),
            scratch_shapes=[
                pltpu.VMEM((total, rows, cols), jnp.bfloat16),
                pltpu.SemaphoreType.DMA((total,)),
            ],
        ),
        compiler_params=pltpu.CompilerParams(vmem_limit_bytes=VMEM_BYTES),
        name="matmul_back",
    )(here.reshape(1), g, *pieces)


def feed_forward(norm_b, cot, pieces, here, down):
    count, width = cot.shape
    total = len(pieces)
    rows, cols = pieces[0].shape
    units = cols // 2
    tile = 2 * LANES

    def kernel(index, x_ref, cot_ref, down_ref, *refs):
        act_ref, grad_ref = refs[total:]
        pair = None
        for mask in range(total):
            start = pl.multiple_of((index[0] ^ mask) * rows, LANES)
            part = jnp.dot(
                x_ref[:, pl.ds(start, rows)], refs[mask][...], preferred_element_type=jnp.float32
            )
            pair = part if pair is None else pair + part
        grad_act = lax.dot_general(
            cot_ref[...],
            down_ref[...],
            (((1,), (1,)), ((), ())),
            preferred_element_type=jnp.float32,
        )
        for k in range(tile // LANES):
            gate = pair[:, 2 * k * LANES : (2 * k + 1) * LANES]
            upval = pair[:, (2 * k + 1) * LANES : (2 * k + 2) * LANES]
            upstream = grad_act[:, k * LANES : (k + 1) * LANES]
            sigma = 1.0 / (1.0 + jnp.exp(-gate))
            silu = gate * sigma
            act_ref[:, k * LANES : (k + 1) * LANES] = (silu * upval).astype(jnp.bfloat16)
            grad_ref[:, 2 * k * LANES : (2 * k + 1) * LANES] = (
                upstream * upval * sigma * (1.0 + gate * (1.0 - sigma))
            ).astype(jnp.bfloat16)
            grad_ref[:, (2 * k + 1) * LANES : (2 * k + 2) * LANES] = (upstream * silu).astype(
                jnp.bfloat16
            )

    return pl.pallas_call(
        kernel,
        out_shape=(
            jax.ShapeDtypeStruct((count, units), jnp.bfloat16),
            jax.ShapeDtypeStruct((count, cols), jnp.bfloat16),
        ),
        grid_spec=pltpu.PrefetchScalarGridSpec(
            num_scalar_prefetch=1,
            grid=(pl.cdiv(units, tile),),
            in_specs=[
                pl.BlockSpec(norm_b.shape, lambda i, s: (0, 0)),
                pl.BlockSpec(cot.shape, lambda i, s: (0, 0)),
                pl.BlockSpec((tile, width), lambda i, s: (i, 0)),
            ]
            + [pl.BlockSpec((rows, 2 * tile), lambda i, s: (0, i))] * total,
            out_specs=(
                pl.BlockSpec((count, tile), lambda i, s: (0, i)),
                pl.BlockSpec((count, 2 * tile), lambda i, s: (0, i)),
            ),
        ),
        compiler_params=pltpu.CompilerParams(vmem_limit_bytes=VMEM_BYTES),
        name="feed_forward",
    )(here.reshape(1), norm_b, cot, down, *pieces)


def weight_blocks(x, g, odd):
    size = lax.axis_size("dp")
    here = lax.axis_index("dp")
    rows = x.shape[1] // size
    blocks = {}
    for mask in range(1 if odd else 0, size, 2):
        cut = lax.dynamic_slice_in_dim(x, (here ^ mask) * rows, rows, 1)
        blocks[mask] = lax.dot_general(
            cut, g, (((0,), (0,)), ((), ())), preferred_element_type=jnp.float32
        )
    return blocks


def row_blocks(partial, odd):
    size = lax.axis_size("dp")
    here = lax.axis_index("dp")
    rows = partial.shape[0] // size
    return {
        mask: lax.dynamic_slice_in_dim(partial, (here ^ mask) * rows, rows, 0)
        for mask in range(1 if odd else 0, size, 2)
    }


def to_partner(blocks):
    return {mask: swap(block.astype(jnp.bfloat16), "dp", 1) for mask, block in blocks.items()}


def with_partner(blocks, got):
    return {mask: block + got[mask | 1].astype(jnp.float32) for mask, block in blocks.items()}


def to_owners(blocks):
    return {
        mask: swap(block.astype(jnp.bfloat16), "dp", mask) if mask else block
        for mask, block in blocks.items()
    }


def total_of(got):
    result = got[0]
    for mask, block in got.items():
        if mask:
            result = result + block.astype(jnp.float32)
    return result


def sum_rows(partial_value):
    return lax.psum_scatter(
        partial_value.astype(jnp.bfloat16), "ctx", scatter_dimension=0, tiled=True
    ).astype(jnp.float32)


def shards(
    layer_input,
    block_table,
    positions,
    first_gain,
    first_shift,
    qkv_weight,
    qkv_bias,
    out_weight,
    second_gain,
    second_shift,
    gate_weight,
    up_weight,
    down_weight,
    cotangent,
):
    count, width = layer_input.shape
    parts = lax.axis_size("ctx")
    groups_dp = lax.axis_size("dp")
    ctx_index = lax.axis_index("ctx")
    dp_index = lax.axis_index("dp")
    quarter = width // parts
    rows_here = first_gain.shape[0]
    bias_here = qkv_bias.shape[0]
    everyone = groups_dp * parts

    small = jnp.concatenate(
        [
            first_gain,
            first_shift,
            second_gain,
            second_shift,
            qkv_bias,
            positions.astype(jnp.float32),
        ]
    )
    small_size = small.shape[0]
    small_rows = -(-small_size // (8 * LANES)) * 8
    small = jnp.pad(small, (0, small_rows * LANES - small_size)).reshape(small_rows, LANES)
    small_line = ctx_gather(small)

    qkv_picked = pick_columns(after(qkv_weight, small), 3, parts, ctx_index)
    qkv_line = ctx_exchange(qkv_picked)

    small_line = stack_rows(after(small_line, qkv_picked), ctx_index, 8)
    small_all = lax.all_gather(small_line, "dp", axis=0, tiled=True)
    small_all = small_all.reshape(everyone, small_rows * LANES)
    gain_one = small_all[:, :rows_here].reshape(width)
    shift_one = small_all[:, rows_here : 2 * rows_here].reshape(width)
    gain_two = small_all[:, 2 * rows_here : 3 * rows_here].reshape(width)
    shift_two = small_all[:, 3 * rows_here : 4 * rows_here].reshape(width)
    bias_full = small_all[:, 4 * rows_here : 4 * rows_here + bias_here]
    bias_full = bias_full.reshape(3, parts, quarter)
    bias_three = lax.dynamic_index_in_dim(bias_full, ctx_index, axis=1, keepdims=False)
    pos_all = small_all[:, 4 * rows_here + bias_here : small_size]
    pos_all = pos_all.reshape(groups_dp, parts * count)
    group_pos = lax.dynamic_index_in_dim(pos_all, dp_index, axis=0, keepdims=False)
    group_pos = group_pos.astype(jnp.int32)
    key_index = logical_index(block_table[0])
    low_index = (key_index - group_pos)[:, None]
    own_index = key_index[:, None]
    key_index = key_index[None, :]
    tables = rotary_tables(group_pos, LANES // HD)
    gate_first, up_first = after((gate_weight, up_weight), small_all)
    pair_picked = pick_units(gate_first, up_first, groups_dp, parts, ctx_index)
    qkv_line = after(qkv_line, pair_picked)

    qkv_block = stack_rows(qkv_line, ctx_index)
    group_input = lax.all_gather(
        after(layer_input, qkv_block), "ctx", axis=0, tiled=True
    )
    qkv_got = gather_first(qkv_block)

    qkv_got, out_rows_own = after((qkv_got, out_weight), tables)
    out_rows_own = after(out_rows_own, *[p for m, p in qkv_got.items() if m])
    out_line = ctx_gather(out_rows_own)
    qkv_got = gather_second(qkv_got)
    second_done = jax.tree.leaves([p for m, p in qkv_got.items() if m and not one_bit(m)])
    pair_line = ctx_exchange(after(pair_picked, *second_done))
    down_got = gather_first(after(down_weight, *second_done))
    qkv_pieces, qkv_here = ready(gather_last(qkv_got), dp_index)

    own_start = ctx_index * count
    inputs = group_input.astype(jnp.float32)
    norm_one, normed_one, inverse_one = layer_norm(inputs, gain_one, shift_one)
    norm_one_b = norm_one.astype(jnp.bfloat16)
    out_block = stack_rows(after(out_line, norm_one_b), ctx_index)
    out_got = gather_first(out_block)
    norm_one_b = after(norm_one_b, out_block)
    proj = matmul_pieces(norm_one_b, qkv_pieces, qkv_here, bias_three.reshape(1, 3 * quarter), 512)
    saved = attend(proj, tables, own_index, low_index, key_index)
    attended = saved[3]
    heads_full = lax.all_gather(attended, "ctx", axis=1, tiled=True)
    group_cot = lax.all_gather(after(cotangent, attended), "ctx", axis=0, tiled=True)

    out_got, pair_line, down_got = after((out_got, pair_line, down_got), attended)
    out_got = gather_second(out_got)
    down_got = gather_second(down_got)
    pair_block = stack_rows(pair_line, ctx_index)
    pair_got = gather_first(pair_block)
    down_pieces = gather_last(after(down_got, pair_block))
    down_part = place(down_pieces, dp_index)
    pair_got = gather_second(pair_got)
    out_pieces, out_here = ready(gather_last(out_got), dp_index)

    mixed = matmul_pieces(heads_full, out_pieces, out_here, group_input, 512)
    pair_got = after(pair_got, mixed)
    pair_pieces, pair_here = ready(gather_last(pair_got), dp_index)
    norm_two, _, _ = layer_norm(mixed, gain_two, shift_two)
    norm_two_b = norm_two.astype(jnp.bfloat16)
    act_b, grad_pair_b = feed_forward(norm_two_b, group_cot, pair_pieces, pair_here, down_part)
    norm_two_part = matmul_back(grad_pair_b, pair_pieces, pair_here)
    grad_two_own = sum_rows(norm_two_part)

    norm_two_late, act_late, grad_pair_late, mixed_late = after(
        (norm_two_b, act_b, grad_pair_b, mixed), norm_two_part
    )
    pair_sent = to_partner(weight_blocks(norm_two_late, grad_pair_late, True))
    mixed_own = lax.dynamic_slice_in_dim(mixed_late, own_start, count, 0)
    _, normed_two_own, inverse_two_own = layer_norm(mixed_own, gain_two, shift_two)
    grad_down = lax.dot_general(
        act_late, group_cot, (((0,), (0,)), ((), ())), preferred_element_type=jnp.float32
    )
    down_sent = to_partner(row_blocks(grad_down, True))
    pair_sums = with_partner(weight_blocks(norm_two_late, grad_pair_late, False), pair_sent)
    pair_way = to_owners(pair_sums)
    act_late = after(act_late, pair_sums)
    feed_part = jnp.dot(act_late, down_part, preferred_element_type=jnp.float32).astype(
        jnp.bfloat16
    )
    down_sums = with_partner(row_blocks(grad_down, False), down_sent)
    down_way = to_owners(down_sums)

    grad_two_own = after(grad_two_own, feed_part, down_sums)
    grad_gain_two = jnp.sum(grad_two_own * normed_two_own, axis=0)
    grad_shift_two = jnp.sum(grad_two_own, axis=0)
    grad_mixed_own = cotangent.astype(jnp.float32) + norm_back(
        grad_two_own, gain_two, normed_two_own, inverse_two_own
    )
    grad_mixed_own_b = grad_mixed_own.astype(jnp.bfloat16)
    grad_mixed_b = lax.all_gather(grad_mixed_own_b, "ctx", axis=0, tiled=True)
    late_pieces = after(out_pieces, grad_mixed_own_b)
    out_rows = rows_of(late_pieces, out_here, ctx_index, quarter)
    feed_part = after(feed_part, grad_mixed_b)
    feed_cut = [
        lax.dynamic_slice_in_dim(feed_part, (ctx_index ^ mask) * count, count, 0)
        for mask in range(parts)
    ]
    feed_line = ctx_exchange(feed_cut)

    grad_proj_b, bias_sums = attend_back(
        saved, grad_mixed_b, out_rows, tables, own_index, low_index, key_index
    )
    bias_spread = lax.dynamic_update_slice_in_dim(
        jnp.zeros((3, parts, quarter), jnp.float32),
        bias_sums.reshape(3, 1, quarter),
        ctx_index,
        1,
    )
    norm_one_part = matmul_back(grad_proj_b, qkv_pieces, qkv_here)
    grad_norm_one = sum_rows(norm_one_part)

    norm_one_late, grad_proj_late, grad_mixed_late = after(
        (norm_one_b, grad_proj_b, grad_mixed_b), norm_one_part
    )
    qkv_odd = weight_blocks(norm_one_late, grad_proj_late, True)
    qkv_sent = to_partner(qkv_odd)
    normed_one_late = after(normed_one, qkv_odd)
    part_f32 = norm_one_part.astype(jnp.float32)
    grad_gain_one = jnp.sum(part_f32 * normed_one_late, axis=0)
    grad_shift_one = jnp.sum(part_f32, axis=0)
    small_grads = jnp.concatenate(
        [
            grad_gain_one.reshape(everyone, rows_here),
            grad_shift_one.reshape(everyone, rows_here),
            grad_gain_two.reshape(everyone, rows_here),
            grad_shift_two.reshape(everyone, rows_here),
            bias_spread.reshape(everyone, bias_here),
        ],
        axis=1,
    )
    small_grads = jnp.pad(
        small_grads, ((0, 0), (0, small_rows * LANES - small_grads.shape[1]))
    ).reshape(everyone * small_rows, LANES)
    small_odd = jnp.concatenate(list(row_blocks(small_grads, True).values()), axis=0)
    small_even = jnp.concatenate(list(row_blocks(small_grads, False).values()), axis=0)
    small_even = small_even + swap(small_odd, "dp", 1)

    mixed_grad_cols = lax.dynamic_slice_in_dim(
        grad_mixed_late, ctx_index * quarter, quarter, 1
    )
    out_sent = to_partner(weight_blocks(heads_full, mixed_grad_cols, True))
    qkv_sums = with_partner(weight_blocks(norm_one_late, grad_proj_late, False), qkv_sent)
    qkv_way = to_owners(qkv_sums)
    small_even = after(small_even, qkv_sums)
    small_block = parts * small_rows
    small_sums = {
        mask: small_even[mask // 2 * small_block : (mask // 2 + 1) * small_block]
        for mask in range(0, groups_dp, 2)
    }
    small_way = [swap(block, "dp", mask) if mask else block for mask, block in small_sums.items()]
    mixed_grad_cols = after(mixed_grad_cols, qkv_sums)
    out_sums = with_partner(weight_blocks(heads_full, mixed_grad_cols, False), out_sent)
    out_way = to_owners(out_sums)

    pair_way, down_way = after((pair_way, down_way), out_sums)
    pair_cut = sum_and_pick(list(pair_way.values()), parts, ctx_index)
    pair_line_own = ctx_exchange(pair_cut)
    down_own = total_of(after(down_way, pair_cut))

    feed_line_late = after(feed_line, pair_cut)
    small_mine = sum(after(small_way, pair_cut))
    small_cut = [
        lax.dynamic_slice_in_dim(small_mine, (ctx_index ^ mask) * small_rows, small_rows, 0)
        for mask in range(parts)
    ]
    small_line_own = ctx_exchange(small_cut)
    qkv_way, out_way = after((qkv_way, out_way), pair_cut, down_own, small_cut)
    qkv_cut = sum_and_pick(list(qkv_way.values()), parts, ctx_index)
    qkv_line_own = ctx_exchange(qkv_cut)
    out_cut = sum_and_pick(list(after(out_way, qkv_cut).values()), parts, ctx_index)
    out_line_own = ctx_exchange(out_cut)
    gate_own, up_own = unpick_units(after(pair_line_own, out_cut), groups_dp, ctx_index)
    normed_one_own = lax.dynamic_slice_in_dim(normed_one, own_start, count, 0)
    inverse_one_own = lax.dynamic_slice_in_dim(inverse_one, own_start, count, 0)
    grad_norm_one = after(grad_norm_one, out_cut)
    grad_input = grad_mixed_own + norm_back(
        grad_norm_one, gain_one, normed_one_own, inverse_one_own
    )
    feed_out = sum(piece.astype(jnp.float32) for piece in feed_line_late)
    layer_output = (mixed_own + feed_out).astype(jnp.bfloat16)
    small_own = sum(after(small_line_own, gate_own)).reshape(small_rows * LANES)
    qkv_own = unpick_columns(qkv_line_own, 3, ctx_index)
    out_own = unpick_columns(out_line_own, 1, ctx_index)
    return (
        layer_output,
        grad_input,
        small_own[:rows_here],
        small_own[rows_here : 2 * rows_here],
        qkv_own,
        small_own[4 * rows_here : 4 * rows_here + bias_here],
        out_own,
        small_own[2 * rows_here : 3 * rows_here],
        small_own[3 * rows_here : 4 * rows_here],
        gate_own,
        up_own,
        down_own,
    )


def solution(mesh):
    return jax.shard_map(
        shards,
        mesh=mesh,
        in_specs=(
            P(("dp", "ctx"), None),
            P("dp", None),
            P(("dp", "ctx")),
            P(("dp", "ctx")),
            P(("dp", "ctx")),
            P(("dp", "ctx"), None),
            P(("dp", "ctx")),
            P(("dp", "ctx"), None),
            P(("dp", "ctx")),
            P(("dp", "ctx")),
            P(("dp", "ctx"), None),
            P(("dp", "ctx"), None),
            P(("dp", "ctx"), None),
            P(("dp", "ctx"), None),
        ),
        out_specs=(
            P(("dp", "ctx"), None),
            P(("dp", "ctx"), None),
            P(("dp", "ctx")),
            P(("dp", "ctx")),
            P(("dp", "ctx"), None),
            P(("dp", "ctx")),
            P(("dp", "ctx"), None),
            P(("dp", "ctx")),
            P(("dp", "ctx")),
            P(("dp", "ctx"), None),
            P(("dp", "ctx"), None),
            P(("dp", "ctx"), None),
        ),
        check_vma=False,
    )
```

```python
import jax
import jax.numpy as jnp
from jax import lax
from jax.experimental import pallas as pl
from jax.experimental.pallas import tpu as pltpu
from jax.sharding import PartitionSpec as P

HD = 64
ROT = 16
BLOCK = 128


EPS = 1e-05


def layer_norm(values, gain, shift):
    average = jnp.mean(values, axis=-1, keepdims=True)
    centred = values - average
    inverse = lax.rsqrt(jnp.mean(centred * centred, axis=-1, keepdims=True) + EPS)
    normed = centred * inverse
    return (normed * gain + shift, normed, inverse)


def norm_back(upstream, gain, normed, inverse):
    scaled = upstream * gain
    centred = scaled - jnp.mean(scaled, axis=-1, keepdims=True)
    return inverse * (centred - normed * jnp.mean(scaled * normed, axis=-1, keepdims=True))


def rotary_tables(token_pos, copies):
    half_rot = ROT // 2
    freqs = 10000.0 ** (-2.0 * jnp.arange(half_rot, dtype=jnp.float32) / ROT)
    angles = token_pos.astype(jnp.float32)[:, None] * freqs[None, :]
    cosine = jnp.cos(angles)
    sine = jnp.sin(angles)
    rest = jnp.zeros((token_pos.shape[0], HD - ROT), jnp.float32)
    zero = jnp.zeros_like(sine)
    keep = jnp.concatenate([cosine, cosine, rest + 1.0], axis=1)
    down = jnp.concatenate([-sine, zero, rest], axis=1)
    up = jnp.concatenate([zero, sine, rest], axis=1)
    return tuple(jnp.concatenate([table] * copies, axis=1) for table in (keep, down, up))


def logical_index(table_row):
    offsets = jnp.tile(jnp.arange(BLOCK, dtype=jnp.int32), table_row.shape[0])
    return jnp.repeat(table_row, BLOCK) * BLOCK + offsets


LANES = 128
VMEM_BYTES = 56 * 1024 * 1024


def after(value, *deps):
    return lax.optimization_barrier((value, deps))[0]


def swap(value, axis, mask):
    return lax.ppermute(value, axis, [(i, i ^ mask) for i in range(lax.axis_size(axis))])


def whole_call(kernel, out_shapes, here, *args, scratch=()):
    return pl.pallas_call(
        kernel,
        out_shape=out_shapes,
        in_specs=[pl.BlockSpec(memory_space=pltpu.SMEM)]
        + [pl.BlockSpec(memory_space=pltpu.VMEM)] * len(args),
        out_specs=jax.tree.map(lambda _: pl.BlockSpec(memory_space=pltpu.VMEM), out_shapes),
        scratch_shapes=list(scratch),
        compiler_params=pltpu.CompilerParams(vmem_limit_bytes=VMEM_BYTES),
    )(here.reshape(1), *args)


def pick_columns(weight, fields, parts, here):
    rows, cols = weight.shape
    wide = cols // (fields * parts)

    def kernel(index, source, *outs):
        for mask in range(parts):
            part = index[0] ^ mask
            for field in range(fields):
                start = pl.multiple_of((field * parts + part) * wide, LANES)
                outs[mask][:, field * wide : (field + 1) * wide] = source[:, pl.ds(start, wide)]

    shape = jax.ShapeDtypeStruct((rows, fields * wide), weight.dtype)
    return list(whole_call(kernel, (shape,) * parts, here, weight))


def unpick_columns(pieces, fields, here):
    parts = len(pieces)
    rows, cols = pieces[0].shape
    wide = cols // fields

    def kernel(index, *refs):
        out = refs[parts]
        for mask in range(parts):
            part = index[0] ^ mask
            for field in range(fields):
                start = pl.multiple_of((field * parts + part) * wide, LANES)
                out[:, pl.ds(start, wide)] = refs[mask][
                    :, field * wide : (field + 1) * wide
                ].astype(jnp.float32)

    shape = jax.ShapeDtypeStruct((rows, parts * cols), jnp.float32)
    return whole_call(kernel, shape, here, *pieces)


def pick_units(gate, up, groups, parts, here):
    rows, hidden = gate.shape
    units = hidden // (groups * parts)
    local = hidden // parts

    def kernel(index, gate_ref, up_ref, *refs):
        outs, scratch = refs[:parts], refs[parts]
        for side, ref in enumerate((gate_ref, up_ref)):
            value = ref[...]
            for part in range(parts):
                mine = jnp.concatenate(
                    [
                        value[:, (g * parts + part) * units : (g * parts + part + 1) * units]
                        for g in range(groups)
                    ],
                    axis=1,
                )
                for k in range(local // LANES):
                    at = (2 * k + side) * LANES
                    scratch[part, :, at : at + LANES] = mine[:, k * LANES : (k + 1) * LANES]
        for mask in range(parts):
            outs[mask][...] = scratch[index[0] ^ mask]

    shape = jax.ShapeDtypeStruct((rows, 2 * local), gate.dtype)
    return list(
        whole_call(
            kernel,
            (shape,) * parts,
            here,
            gate,
            up,
            scratch=[pltpu.VMEM((parts, rows, 2 * local), gate.dtype)],
        )
    )


def unpick_units(pieces, groups, here):
    parts = len(pieces)
    rows, cols = pieces[0].shape
    local = cols // 2
    units = local // groups

    def kernel(index, *refs):
        outs, scratch = refs[parts : parts + 2], refs[parts + 2]
        for mask in range(parts):
            scratch[index[0] ^ mask] = refs[mask][...].astype(jnp.float32)
        for side in range(2):
            mine = []
            for part in range(parts):
                mine.append(
                    jnp.concatenate(
                        [
                            scratch[part, :, (2 * k + side) * LANES : (2 * k + side + 1) * LANES]
                            for k in range(local // LANES)
                        ],
                        axis=1,
                    )
                )
            outs[side][...] = jnp.concatenate(
                [
                    mine[part][:, g * units : (g + 1) * units]
                    for g in range(groups)
                    for part in range(parts)
                ],
                axis=1,
            )

    shape = jax.ShapeDtypeStruct((rows, local * parts), jnp.float32)
    return whole_call(
        kernel,
        (shape, shape),
        here,
        *pieces,
        scratch=[pltpu.VMEM((parts, rows, cols), jnp.float32)],
    )


def stack_rows(pieces, here, aligned=16):
    parts = len(pieces)
    rows, cols = pieces[0].shape

    def kernel(index, *refs):
        for mask in range(parts):
            start = pl.multiple_of((index[0] ^ mask) * rows, aligned)
            refs[parts][pl.ds(start, rows), :] = refs[mask][...]

    shape = jax.ShapeDtypeStruct((parts * rows, cols), pieces[0].dtype)
    return whole_call(kernel, shape, here, *pieces)


def sum_and_pick(blocks, parts, here):
    total = len(blocks)
    rows, cols = blocks[0].shape
    rows = rows // parts

    def kernel(index, *refs):
        for mask in range(parts):
            start = pl.multiple_of((index[0] ^ mask) * rows, 16)
            value = refs[0][pl.ds(start, rows), :].astype(jnp.float32)
            for k in range(1, total):
                value = value + refs[k][pl.ds(start, rows), :].astype(jnp.float32)
            refs[total + mask][...] = value.astype(jnp.bfloat16)

    shape = jax.ShapeDtypeStruct((rows, cols), jnp.bfloat16)
    return list(whole_call(kernel, (shape,) * parts, here, *blocks))


def rotated(field, tables):
    half_rot = ROT // 2
    keep, down, up = tables
    lanes = field.shape[1]
    return (
        field * keep
        + pltpu.roll(field, lanes - half_rot, 1) * down
        + pltpu.roll(field, half_rot, 1) * up
    )


def mask_of(own_ref, low_ref, key_ref):
    return (key_ref[...] <= own_ref[...]) & (key_ref[...] >= low_ref[...])


def probabilities(query, key, visible):
    scores = lax.dot_general(
        query, key, (((1,), (1,)), ((), ())), preferred_element_type=jnp.float32
    ) * HD ** (-0.5)
    total = jnp.sum(jnp.where(visible, jnp.exp(scores), 0.0), axis=1, keepdims=True)
    return jnp.where(visible, jnp.exp(scores - jnp.log(total)), 0.0)


def attend(proj, tables, own_index, low_index, key_index):
    count, cols = proj.shape
    quarter = cols // 3
    steps = quarter // LANES

    def kernel(q_ref, k_ref, v_ref, c_ref, s_ref, t_ref, own, low, keys, qo, ko, vo, att):
        tables_here = (c_ref[...], s_ref[...], t_ref[...])
        query = rotated(q_ref[...], tables_here).astype(jnp.bfloat16)
        key = rotated(k_ref[...], tables_here).astype(jnp.bfloat16)
        value = v_ref[...].astype(jnp.bfloat16)
        qo[...] = query
        ko[...] = key
        vo[...] = value
        visible = mask_of(own, low, keys)
        for h in range(LANES // HD):
            cut = slice(h * HD, (h + 1) * HD)
            prob_b = probabilities(query[:, cut], key[:, cut], visible).astype(jnp.bfloat16)
            att[:, cut] = jnp.dot(
                prob_b, value[:, cut], preferred_element_type=jnp.float32
            ).astype(jnp.bfloat16)

    tile = pl.BlockSpec((count, LANES), lambda i: (0, i))
    full = pl.BlockSpec((count, LANES), lambda i: (0, 0))
    column = pl.BlockSpec((count, 1), lambda i: (0, 0))
    shape = jax.ShapeDtypeStruct((count, quarter), jnp.bfloat16)
    return pl.pallas_call(
        kernel,
        out_shape=(shape,) * 4,
        grid=(steps,),
        in_specs=[
            tile,
            pl.BlockSpec((count, LANES), lambda i: (0, i + steps)),
            pl.BlockSpec((count, LANES), lambda i: (0, i + 2 * steps)),
            full,
            full,
            full,
            column,
            column,
            pl.BlockSpec((1, count), lambda i: (0, 0)),
        ],
        out_specs=(tile,) * 4,
        compiler_params=pltpu.CompilerParams(vmem_limit_bytes=VMEM_BYTES),
        name="attend",
    )(proj, proj, proj, *tables, own_index, low_index, key_index)


def attend_back(saved, grad_mixed_b, out_rows, tables, own_index, low_index, key_index):
    query_all, key_all, value_all, attended = saved
    count, quarter = query_all.shape
    width = grad_mixed_b.shape[1]
    steps = quarter // LANES

    def kernel(q_ref, k_ref, v_ref, a_ref, g_ref, w_ref, c_ref, s_ref, t_ref, own, low, keys, out, sums):
        step = pl.program_id(0)
        visible = mask_of(own, low, keys)
        back = (c_ref[...], -s_ref[...], -t_ref[...])
        grad_att = lax.dot_general(
            g_ref[...], w_ref[...], (((1,), (1,)), ((), ())), preferred_element_type=jnp.float32
        ).astype(jnp.bfloat16)
        products = grad_att.astype(jnp.float32) * a_ref[...].astype(jnp.float32)
        query = q_ref[...]
        key = k_ref[...]
        value = v_ref[...]
        grads = ([], [], [])
        for h in range(LANES // HD):
            cut = slice(h * HD, (h + 1) * HD)
            prob = probabilities(query[:, cut], key[:, cut], visible)
            grad_value = lax.dot_general(
                prob.astype(jnp.bfloat16),
                grad_att[:, cut],
                (((0,), (0,)), ((), ())),
                preferred_element_type=jnp.float32,
            )
            grad_prob = lax.dot_general(
                grad_att[:, cut],
                value[:, cut],
                (((1,), (1,)), ((), ())),
                preferred_element_type=jnp.float32,
            )
            delta = jnp.sum(products[:, cut], axis=1, keepdims=True)
            grad_scores = (prob * (grad_prob - delta) * HD ** (-0.5)).astype(jnp.bfloat16)
            grads[0].append(
                jnp.dot(grad_scores, key[:, cut], preferred_element_type=jnp.float32)
            )
            grads[1].append(
                lax.dot_general(
                    grad_scores,
                    query[:, cut],
                    (((0,), (0,)), ((), ())),
                    preferred_element_type=jnp.float32,
                )
            )
            grads[2].append(grad_value)
        for field in range(3):
            grad = jnp.concatenate(grads[field], axis=1)
            if field < 2:
                grad = rotated(grad, back)
            start = pl.multiple_of(field * quarter + step * LANES, LANES)
            out[:, pl.ds(start, LANES)] = grad.astype(jnp.bfloat16)
            sums[:, pl.ds(start, LANES)] = jnp.sum(grad, axis=0, keepdims=True)

    tile = pl.BlockSpec((count, LANES), lambda i: (0, i))
    full = pl.BlockSpec((count, LANES), lambda i: (0, 0))
    column = pl.BlockSpec((count, 1), lambda i: (0, 0))
    return pl.pallas_call(
        kernel,
        out_shape=(
            jax.ShapeDtypeStruct((count, 3 * quarter), jnp.bfloat16),
            jax.ShapeDtypeStruct((1, 3 * quarter), jnp.float32),
        ),
        grid=(steps,),
        in_specs=[tile] * 4
        + [
            pl.BlockSpec((count, width), lambda i: (0, 0)),
            pl.BlockSpec((LANES, width), lambda i: (i, 0)),
            full,
            full,
            full,
            column,
            column,
            pl.BlockSpec((1, count), lambda i: (0, 0)),
        ],
        out_specs=(
            pl.BlockSpec((count, 3 * quarter), lambda i: (0, 0)),
            pl.BlockSpec((1, 3 * quarter), lambda i: (0, 0)),
        ),
        compiler_params=pltpu.CompilerParams(vmem_limit_bytes=VMEM_BYTES),
        name="attend_back",
    )(
        query_all,
        key_all,
        value_all,
        attended,
        grad_mixed_b,
        out_rows,
        *tables,
        own_index,
        low_index,
        key_index,
    )


def rows_of(pieces, here, part, wide):
    total = len(pieces)
    rows, cols = pieces[0].shape
    if total == 1:
        return lax.dynamic_slice_in_dim(pieces[0], part * wide, wide, 0)
    per = wide // rows

    def kernel(index, *refs):
        out, sem = refs[total], refs[total + 1]
        for mask in range(total):
            block = index[0] ^ mask

            @pl.when(block // per == index[1])
            def _(mask=mask, block=block):
                start = pl.multiple_of((block % per) * rows, 16)
                copy = pltpu.make_async_copy(refs[mask], out.at[pl.ds(start, rows), :], sem)
                copy.start()
                copy.wait()

    return pl.pallas_call(
        kernel,
        out_shape=jax.ShapeDtypeStruct((wide, cols), pieces[0].dtype),
        in_specs=[pl.BlockSpec(memory_space=pltpu.SMEM)]
        + [pl.BlockSpec(memory_space=pl.ANY)] * total,
        out_specs=pl.BlockSpec(memory_space=pltpu.VMEM),
        scratch_shapes=[pltpu.SemaphoreType.DMA],
        compiler_params=pltpu.CompilerParams(vmem_limit_bytes=VMEM_BYTES),
        name="rows_of",
    )(jnp.stack([here, part]), *pieces)


def place(pieces, here):
    rows, cols = pieces[0].shape
    result = jnp.zeros((len(pieces) * rows, cols), pieces[0].dtype)
    for mask, piece in enumerate(pieces):
        result = lax.dynamic_update_slice(result, piece, ((here ^ mask) * rows, 0))
    return result


def ctx_exchange(picked):
    return picked[:1] + [swap(picked[mask], "ctx", mask) for mask in range(1, len(picked))]


def ctx_gather(rows_own):
    return [rows_own] + [
        swap(rows_own, "ctx", mask) for mask in range(1, lax.axis_size("ctx"))
    ]


def one_bit(mask):
    return mask & (mask - 1) == 0


def gather_first(block):
    size = lax.axis_size("dp")
    got = {0: block}
    for mask in range(2, size, 2):
        if one_bit(mask):
            got[mask] = swap(block, "dp", mask)
    return got


def gather_second(got):
    size = lax.axis_size("dp")
    got = dict(got)
    rows = got[0].shape[0]
    half = rows // 16 * 8
    for mask in range(2, size, 2):
        if one_bit(mask):
            continue
        low = mask & -mask
        high = mask ^ low
        if one_bit(high):
            got[mask] = (
                swap(got[low][:half], "dp", high),
                swap(got[high][half:], "dp", low),
            )
        else:
            got[mask] = swap(got[0], "dp", mask)
    return got


def gather_last(got):
    size = lax.axis_size("dp")
    pieces = []
    for mask in range(0, size, 2):
        mine = got[mask]
        if isinstance(mine, tuple):
            theirs = tuple(swap(piece, "dp", 1) for piece in mine)
            pieces.append(jnp.concatenate(mine, axis=0))
            pieces.append(jnp.concatenate(theirs, axis=0))
        else:
            pieces.append(mine)
            pieces.append(swap(mine, "dp", 1))
    return pieces


def ready(pieces, here):
    if pieces[0].shape[0] % LANES == 0:
        return pieces, here
    return [place(pieces, here)], jnp.zeros_like(here)


def tile_of(cols, most):
    best = LANES
    for tile in range(LANES, most + 1, LANES):
        if cols % tile == 0:
            best = tile
    return best


def normalize(source, gain, shift, *targets):
    count = source.shape[0]
    chunk = min(64, count)

    def some(i, _):
        rows = pl.ds(pl.multiple_of(i * chunk, 16), chunk)
        norm = layer_norm(source[rows, :].astype(jnp.float32), gain[...], shift[...])[0]
        for target in targets:
            target[rows, :] = norm.astype(jnp.bfloat16)
        return 0

    lax.fori_loop(0, count // chunk, some, 0)


def matmul_pieces(x, pieces, here, added, most, norm=None):
    count, width = x.shape
    total = len(pieces)
    rows, cols = pieces[0].shape
    tile = tile_of(cols, most)

    def kernel(index, x_ref, added_ref, *refs):
        weights = refs[:total]
        source = x_ref
        if norm:
            gain, shift, out, normed, source = refs[total:]

            @pl.when(pl.program_id(0) == 0)
            def _():
                normalize(x_ref, gain, shift, normed, source)

        else:
            (out,) = refs[total:]
        acc = added_ref[...].astype(jnp.float32)
        for mask in range(total):
            start = pl.multiple_of((index[0] ^ mask) * rows, LANES)
            acc = acc + jnp.dot(
                source[:, pl.ds(start, rows)],
                weights[mask][...],
                preferred_element_type=jnp.float32,
            )
        out[...] = acc

    full = pl.BlockSpec(x.shape, lambda i, s: (0, 0))
    vector = pl.BlockSpec((1, width), lambda i, s: (0, 0))
    out_shape = [jax.ShapeDtypeStruct((count, cols), jnp.float32)]
    out_specs = [pl.BlockSpec((count, tile), lambda i, s: (0, i))]
    if norm:
        out_shape.append(jax.ShapeDtypeStruct(x.shape, jnp.bfloat16))
        out_specs.append(full)
    got = pl.pallas_call(
        kernel,
        out_shape=out_shape,
        grid_spec=pltpu.PrefetchScalarGridSpec(
            num_scalar_prefetch=1,
            grid=(cols // tile,),
            in_specs=[full, pl.BlockSpec((added.shape[0], tile), lambda i, s: (0, i))]
            + [pl.BlockSpec((rows, tile), lambda i, s: (0, i))] * total
            + ([vector] * 2 if norm else []),
            out_specs=out_specs,
            scratch_shapes=[pltpu.VMEM(x.shape, jnp.bfloat16)] if norm else [],
        ),
        compiler_params=pltpu.CompilerParams(vmem_limit_bytes=VMEM_BYTES),
        name="matmul_pieces",
    )(here.reshape(1), x, added, *pieces, *(v.reshape(1, width) for v in norm or ()))
    return got if norm else got[0]


def matmul_back(g, pieces, here):
    count, cols = g.shape
    total = len(pieces)
    rows = pieces[0].shape[0]
    ahead = min(2, total)

    def kernel(index, g_ref, *refs):
        out, buffer, sem = refs[total:]

        def fetch(mask):
            pltpu.make_async_copy(refs[mask], buffer.at[mask], sem.at[mask]).start()

        for mask in range(ahead):
            fetch(mask)

        def one(mask, _):
            for k in range(ahead, total):
                pl.when(mask == k - ahead)(lambda k=k: fetch(k))
            pltpu.make_async_copy(refs[0], buffer.at[mask], sem.at[mask]).wait()
            part = lax.dot_general(
                g_ref[...],
                buffer[mask],
                (((1,), (1,)), ((), ())),
                preferred_element_type=jnp.float32,
            )
            start = pl.multiple_of((index[0] ^ mask) * rows, LANES)
            out[:, pl.ds(start, rows)] = part.astype(jnp.bfloat16)
            return 0

        lax.fori_loop(0, total, one, 0)

    return pl.pallas_call(
        kernel,
        out_shape=jax.ShapeDtypeStruct((count, total * rows), jnp.bfloat16),
        grid_spec=pltpu.PrefetchScalarGridSpec(
            num_scalar_prefetch=1,
            grid=(1,),
            in_specs=[pl.BlockSpec(g.shape, lambda i, s: (0, 0))]
            + [pl.BlockSpec(memory_space=pl.ANY)] * total,
            out_specs=pl.BlockSpec((count, total * rows), lambda i, s: (0, 0)),
            scratch_shapes=[
                pltpu.VMEM((total, rows, cols), jnp.bfloat16),
                pltpu.SemaphoreType.DMA((total,)),
            ],
        ),
        compiler_params=pltpu.CompilerParams(vmem_limit_bytes=VMEM_BYTES),
        name="matmul_back",
    )(here.reshape(1), g, *pieces)


def weight_odd(x, g, here, part, wide):
    size = lax.axis_size("dp")
    count, width = x.shape
    rows = width // size
    half = size // 2

    def kernel(index, x_ref, g_ref, out):
        block = index[0] ^ (2 * pl.program_id(0) + 1)
        cut = x_ref[:, pl.ds(pl.multiple_of(block * rows, LANES), rows)]
        out[...] = lax.dot_general(
            cut, g_ref[...], (((0,), (0,)), ((), ())), preferred_element_type=jnp.float32
        ).astype(jnp.bfloat16)

    if rows % LANES:
        g = lax.dynamic_slice_in_dim(g, part * wide, wide, 1)
        blocks = weight_blocks(x, g, True)
        return jnp.concatenate([b.astype(jnp.bfloat16) for b in blocks.values()], axis=0)
    return pl.pallas_call(
        kernel,
        out_shape=jax.ShapeDtypeStruct((half * rows, wide), jnp.bfloat16),
        grid_spec=pltpu.PrefetchScalarGridSpec(
            num_scalar_prefetch=1,
            grid=(half,),
            in_specs=[
                pl.BlockSpec(x.shape, lambda i, s: (0, 0)),
                pl.BlockSpec((count, wide), lambda i, s: (0, s[1])),
            ],
            out_specs=pl.BlockSpec((rows, wide), lambda i, s: (i, 0)),
        ),
        compiler_params=pltpu.CompilerParams(vmem_limit_bytes=VMEM_BYTES),
        name="weight_odd",
    )(jnp.stack([here, part]), x, g)


def weight_even(x, g, here, part, wide, got):
    size = lax.axis_size("dp")
    count, width = x.shape
    rows = width // size
    half = size // 2

    def kernel(index, x_ref, g_ref, got_ref, *outs):
        step = pl.program_id(0)
        block = index[0] ^ (2 * step)
        cut = x_ref[:, pl.ds(pl.multiple_of(block * rows, LANES), rows)]
        value = lax.dot_general(
            cut, g_ref[...], (((0,), (0,)), ((), ())), preferred_element_type=jnp.float32
        ) + got_ref[...].astype(jnp.float32)
        for k in range(half):

            @pl.when(step == k)
            def _(k=k):
                outs[k][...] = value.astype(outs[k].dtype)

    if rows % LANES:
        g = lax.dynamic_slice_in_dim(g, part * wide, wide, 1)
        blocks = weight_blocks(x, g, False)
        return [
            b + got[k * rows : (k + 1) * rows].astype(jnp.float32)
            for k, b in enumerate(blocks.values())
        ]
    return list(
        pl.pallas_call(
            kernel,
            out_shape=[
                jax.ShapeDtypeStruct((rows, wide), jnp.bfloat16 if k else jnp.float32)
                for k in range(half)
            ],
            grid_spec=pltpu.PrefetchScalarGridSpec(
                num_scalar_prefetch=1,
                grid=(half,),
                in_specs=[
                    pl.BlockSpec(x.shape, lambda i, s: (0, 0)),
                    pl.BlockSpec((count, wide), lambda i, s: (0, s[1])),
                    pl.BlockSpec((rows, wide), lambda i, s: (i, 0)),
                ],
                out_specs=[pl.BlockSpec((rows, wide), lambda i, s: (0, 0))] * half,
            ),
            compiler_params=pltpu.CompilerParams(vmem_limit_bytes=VMEM_BYTES),
            name="weight_even",
        )(jnp.stack([here, part]), x, g, got)
    )


def feed_forward(mixed, gain, shift, cot, pieces, here, down):
    count, width = cot.shape
    total = len(pieces)
    rows, cols = pieces[0].shape
    units = cols // 2
    tile = 2 * LANES

    def kernel(index, mixed_ref, gain_ref, shift_ref, cot_ref, down_ref, *refs):
        norm_ref, act_ref, grad_ref, x_ref = refs[total:]

        @pl.when(pl.program_id(0) == 0)
        def _():
            normalize(mixed_ref, gain_ref, shift_ref, norm_ref, x_ref)

        pair = None
        for mask in range(total):
            start = pl.multiple_of((index[0] ^ mask) * rows, LANES)
            part = jnp.dot(
                x_ref[:, pl.ds(start, rows)], refs[mask][...], preferred_element_type=jnp.float32
            )
            pair = part if pair is None else pair + part
        grad_act = lax.dot_general(
            cot_ref[...],
            down_ref[...],
            (((1,), (1,)), ((), ())),
            preferred_element_type=jnp.float32,
        )
        for k in range(tile // LANES):
            gate = pair[:, 2 * k * LANES : (2 * k + 1) * LANES]
            upval = pair[:, (2 * k + 1) * LANES : (2 * k + 2) * LANES]
            upstream = grad_act[:, k * LANES : (k + 1) * LANES]
            sigma = 1.0 / (1.0 + jnp.exp(-gate))
            silu = gate * sigma
            act_ref[:, k * LANES : (k + 1) * LANES] = (silu * upval).astype(jnp.bfloat16)
            grad_ref[:, 2 * k * LANES : (2 * k + 1) * LANES] = (
                upstream * upval * sigma * (1.0 + gate * (1.0 - sigma))
            ).astype(jnp.bfloat16)
            grad_ref[:, (2 * k + 1) * LANES : (2 * k + 2) * LANES] = (upstream * silu).astype(
                jnp.bfloat16
            )

    return pl.pallas_call(
        kernel,
        out_shape=(
            jax.ShapeDtypeStruct((count, width), jnp.bfloat16),
            jax.ShapeDtypeStruct((count, units), jnp.bfloat16),
            jax.ShapeDtypeStruct((count, cols), jnp.bfloat16),
        ),
        grid_spec=pltpu.PrefetchScalarGridSpec(
            num_scalar_prefetch=1,
            grid=(pl.cdiv(units, tile),),
            in_specs=[
                pl.BlockSpec(mixed.shape, lambda i, s: (0, 0)),
                pl.BlockSpec((1, width), lambda i, s: (0, 0)),
                pl.BlockSpec((1, width), lambda i, s: (0, 0)),
                pl.BlockSpec(cot.shape, lambda i, s: (0, 0)),
                pl.BlockSpec((tile, width), lambda i, s: (i, 0)),
            ]
            + [pl.BlockSpec((rows, 2 * tile), lambda i, s: (0, i))] * total,
            out_specs=(
                pl.BlockSpec((count, width), lambda i, s: (0, 0)),
                pl.BlockSpec((count, tile), lambda i, s: (0, i)),
                pl.BlockSpec((count, 2 * tile), lambda i, s: (0, i)),
            ),
            scratch_shapes=[pltpu.VMEM((count, width), jnp.bfloat16)],
        ),
        compiler_params=pltpu.CompilerParams(vmem_limit_bytes=VMEM_BYTES),
        name="feed_forward",
    )(
        here.reshape(1), mixed, gain.reshape(1, width), shift.reshape(1, width), cot, down, *pieces
    )


def weight_blocks(x, g, odd):
    size = lax.axis_size("dp")
    here = lax.axis_index("dp")
    rows = x.shape[1] // size
    blocks = {}
    for mask in range(1 if odd else 0, size, 2):
        cut = lax.dynamic_slice_in_dim(x, (here ^ mask) * rows, rows, 1)
        blocks[mask] = lax.dot_general(
            cut, g, (((0,), (0,)), ((), ())), preferred_element_type=jnp.float32
        )
    return blocks


def row_blocks(partial, odd):
    size = lax.axis_size("dp")
    here = lax.axis_index("dp")
    rows = partial.shape[0] // size
    return {
        mask: lax.dynamic_slice_in_dim(partial, (here ^ mask) * rows, rows, 0)
        for mask in range(1 if odd else 0, size, 2)
    }


def to_owners(blocks):
    return [
        swap(block.astype(jnp.bfloat16), "dp", 2 * k) if k else block
        for k, block in enumerate(blocks)
    ]


def total_of(got):
    result = got[0]
    for block in got[1:]:
        result = result + block.astype(jnp.float32)
    return result


def sum_rows(partial_value):
    return lax.psum_scatter(
        partial_value.astype(jnp.bfloat16), "ctx", scatter_dimension=0, tiled=True
    )


def shards(
    layer_input,
    block_table,
    positions,
    first_gain,
    first_shift,
    qkv_weight,
    qkv_bias,
    out_weight,
    second_gain,
    second_shift,
    gate_weight,
    up_weight,
    down_weight,
    cotangent,
):
    count, width = layer_input.shape
    parts = lax.axis_size("ctx")
    groups_dp = lax.axis_size("dp")
    ctx_index = lax.axis_index("ctx")
    dp_index = lax.axis_index("dp")
    quarter = width // parts
    rows_here = first_gain.shape[0]
    bias_here = qkv_bias.shape[0]
    everyone = groups_dp * parts

    small = jnp.concatenate(
        [
            first_gain,
            first_shift,
            second_gain,
            second_shift,
            qkv_bias,
            positions.astype(jnp.float32),
        ]
    )
    small_size = small.shape[0]
    small_rows = -(-small_size // (8 * LANES)) * 8
    small = jnp.pad(small, (0, small_rows * LANES - small_size)).reshape(small_rows, LANES)
    small_line = ctx_gather(small)

    qkv_picked = pick_columns(after(qkv_weight, small), 3, parts, ctx_index)
    qkv_line = ctx_exchange(qkv_picked)

    small_line = stack_rows(after(small_line, qkv_picked), ctx_index, 8)
    small_all = lax.all_gather(small_line, "dp", axis=0, tiled=True)
    small_all = small_all.reshape(everyone, small_rows * LANES)
    gain_one = small_all[:, :rows_here].reshape(width)
    shift_one = small_all[:, rows_here : 2 * rows_here].reshape(width)
    gain_two = small_all[:, 2 * rows_here : 3 * rows_here].reshape(width)
    shift_two = small_all[:, 3 * rows_here : 4 * rows_here].reshape(width)
    bias_full = small_all[:, 4 * rows_here : 4 * rows_here + bias_here]
    bias_full = bias_full.reshape(3, parts, quarter)
    bias_three = lax.dynamic_index_in_dim(bias_full, ctx_index, axis=1, keepdims=False)
    pos_all = small_all[:, 4 * rows_here + bias_here : small_size]
    pos_all = pos_all.reshape(groups_dp, parts * count)
    group_pos = lax.dynamic_index_in_dim(pos_all, dp_index, axis=0, keepdims=False)
    group_pos = group_pos.astype(jnp.int32)
    key_index = logical_index(block_table[0])
    low_index = (key_index - group_pos)[:, None]
    own_index = key_index[:, None]
    key_index = key_index[None, :]
    tables = rotary_tables(group_pos, LANES // HD)
    gate_first, up_first = after((gate_weight, up_weight), small_all)
    pair_picked = pick_units(gate_first, up_first, groups_dp, parts, ctx_index)
    qkv_line = after(qkv_line, pair_picked)

    qkv_block = stack_rows(qkv_line, ctx_index)
    group_input = lax.all_gather(after(layer_input, qkv_block), "ctx", axis=0, tiled=True)
    qkv_got = gather_first(qkv_block)

    qkv_got, out_rows_own = after((qkv_got, out_weight), tables)
    out_rows_own = after(out_rows_own, *[p for m, p in qkv_got.items() if m])
    out_line = ctx_gather(out_rows_own)
    qkv_got = gather_second(qkv_got)
    second_done = jax.tree.leaves([p for m, p in qkv_got.items() if m and not one_bit(m)])
    pair_line = ctx_exchange(after(pair_picked, *second_done))
    down_got = gather_first(after(down_weight, *second_done))
    qkv_pieces, qkv_here = ready(gather_last(qkv_got), dp_index)
    down_got = after(down_got, *qkv_pieces[:-1])
    down_got = gather_second(down_got)
    out_line = after(out_line, *[p for m, p in down_got.items() if m and one_bit(m)])
    out_block = stack_rows(out_line, ctx_index)
    out_got = gather_first(out_block)

    own_start = ctx_index * count
    group_input = after(group_input, out_block)
    proj, norm_one_b = matmul_pieces(
        group_input,
        qkv_pieces,
        qkv_here,
        bias_three.reshape(1, 3 * quarter),
        512,
        (gain_one, shift_one),
    )
    group_cot = lax.all_gather(after(cotangent, group_input), "ctx", axis=0, tiled=True)
    saved = attend(proj, tables, own_index, low_index, key_index)
    attended = saved[3]
    heads_full = lax.all_gather(attended, "ctx", axis=1, tiled=True)

    out_got, pair_line, down_got = after((out_got, pair_line, down_got), attended)
    pair_block = stack_rows(pair_line, ctx_index)
    pair_got = gather_first(pair_block)
    out_got = gather_second(after(out_got, pair_block))
    down_pieces = gather_last(after(down_got, pair_block))
    down_part = place(down_pieces, dp_index)
    pair_got = gather_second(pair_got)
    out_pieces, out_here = ready(gather_last(out_got), dp_index)

    mixed = matmul_pieces(heads_full, out_pieces, out_here, group_input, 512)
    pair_got = after(pair_got, mixed)
    pair_pieces, pair_here = ready(gather_last(pair_got), dp_index)
    norm_two_b, act_b, grad_pair_b = feed_forward(
        mixed, gain_two, shift_two, group_cot, pair_pieces, pair_here, down_part
    )
    norm_two_part = matmul_back(grad_pair_b, pair_pieces, pair_here)
    grad_two_own = sum_rows(norm_two_part)

    zero = jnp.zeros_like(ctx_index)
    norm_two_late, act_late, grad_pair_late, mixed_late = after(
        (norm_two_b, act_b, grad_pair_b, mixed), norm_two_part
    )
    pair_wide = grad_pair_b.shape[1]
    pair_odd = weight_odd(norm_two_late, grad_pair_late, dp_index, zero, pair_wide)
    pair_sent = swap(pair_odd, "dp", 1)
    act_late, mixed_late = after((act_late, mixed_late), pair_odd)
    mixed_own = lax.dynamic_slice_in_dim(mixed_late, own_start, count, 0)
    _, normed_two_own, inverse_two_own = layer_norm(mixed_own, gain_two, shift_two)
    feed_part = jnp.dot(act_late, down_part, preferred_element_type=jnp.float32).astype(
        jnp.bfloat16
    )
    pair_sent = after(pair_sent, feed_part)
    pair_sums = weight_even(
        norm_two_late, grad_pair_late, dp_index, zero, pair_wide, pair_sent
    )
    pair_way = to_owners(pair_sums)
    act_late = after(act_late, *pair_sums)
    grad_down = lax.dot_general(
        act_late, group_cot, (((0,), (0,)), ((), ())), preferred_element_type=jnp.float32
    )
    down_odd = jnp.concatenate(
        [block.astype(jnp.bfloat16) for block in row_blocks(grad_down, True).values()], axis=0
    )
    down_sent = swap(down_odd, "dp", 1)
    down_rows = down_weight.shape[0]
    down_sums = [
        block + down_sent[k * down_rows : (k + 1) * down_rows].astype(jnp.float32)
        for k, block in enumerate(row_blocks(grad_down, False).values())
    ]
    down_sums = [block.astype(jnp.bfloat16) if k else block for k, block in enumerate(down_sums)]

    grad_two_own = after(grad_two_own, feed_part, down_odd).astype(jnp.float32)
    grad_gain_two = jnp.sum(grad_two_own * normed_two_own, axis=0)
    grad_shift_two = jnp.sum(grad_two_own, axis=0)
    grad_mixed_own = cotangent.astype(jnp.float32) + norm_back(
        grad_two_own, gain_two, normed_two_own, inverse_two_own
    )
    grad_mixed_own_b = grad_mixed_own.astype(jnp.bfloat16)
    grad_mixed_b = lax.all_gather(grad_mixed_own_b, "ctx", axis=0, tiled=True)

    late_pieces, down_sums = after((out_pieces, down_sums), grad_mixed_own_b)
    out_rows = rows_of(late_pieces, out_here, ctx_index, quarter)
    pair_way = after(pair_way, out_rows, down_sums)
    pair_cut = sum_and_pick(pair_way, parts, ctx_index)
    pair_line_own = ctx_exchange(pair_cut)
    down_way = to_owners(after(down_sums, pair_cut))
    feed_part = after(feed_part, grad_mixed_b)
    feed_out = sum_rows(feed_part)

    grad_proj_b, bias_sums = attend_back(
        saved,
        after(grad_mixed_b, pair_cut),
        out_rows,
        tables,
        own_index,
        low_index,
        key_index,
    )
    qkv_wide = 3 * quarter
    qkv_odd = weight_odd(norm_one_b, grad_proj_b, dp_index, zero, qkv_wide)
    qkv_sent = swap(qkv_odd, "dp", 1)
    norm_one_part = matmul_back(after(grad_proj_b, qkv_odd), qkv_pieces, qkv_here)
    grad_norm_one = sum_rows(norm_one_part)

    qkv_sent = after(qkv_sent, norm_one_part)
    qkv_sums = weight_even(norm_one_b, grad_proj_b, dp_index, zero, qkv_wide, qkv_sent)
    qkv_way = to_owners(qkv_sums)
    out_odd = weight_odd(after(heads_full, *qkv_sums), grad_mixed_b, dp_index, ctx_index, quarter)
    out_sent = swap(out_odd, "dp", 1)

    normed_one_late = layer_norm(
        after(group_input, out_odd).astype(jnp.float32), gain_one, shift_one
    )[1]
    bias_spread = lax.dynamic_update_slice_in_dim(
        jnp.zeros((3, parts, quarter), jnp.float32),
        after(bias_sums, out_odd).reshape(3, 1, quarter),
        ctx_index,
        1,
    )
    part_f32 = norm_one_part.astype(jnp.float32)
    grad_gain_one = jnp.sum(part_f32 * normed_one_late, axis=0)
    grad_shift_one = jnp.sum(part_f32, axis=0)
    small_grads = jnp.concatenate(
        [
            grad_gain_one.reshape(everyone, rows_here),
            grad_shift_one.reshape(everyone, rows_here),
            grad_gain_two.reshape(everyone, rows_here),
            grad_shift_two.reshape(everyone, rows_here),
            bias_spread.reshape(everyone, bias_here),
            jnp.zeros((everyone, small_rows * LANES - 4 * rows_here - bias_here), jnp.float32),
        ],
        axis=1,
    ).reshape(everyone * small_rows, LANES)
    small_odd = jnp.concatenate(list(row_blocks(small_grads, True).values()), axis=0)
    small_even = jnp.concatenate(list(row_blocks(small_grads, False).values()), axis=0)
    small_even = small_even + swap(small_odd, "dp", 1)
    small_block = parts * small_rows
    small_sums = [
        small_even[k * small_block : (k + 1) * small_block] for k in range(groups_dp // 2)
    ]
    small_way = [swap(block, "dp", 2 * k) if k else block for k, block in enumerate(small_sums)]
    out_sums = weight_even(
        heads_full,
        grad_mixed_b,
        dp_index,
        ctx_index,
        quarter,
        after(out_sent, *small_sums),
    )
    out_way = to_owners(out_sums)

    qkv_way = after(qkv_way, *out_sums)
    qkv_cut = sum_and_pick(qkv_way, parts, ctx_index)
    qkv_line_own = ctx_exchange(qkv_cut)
    small_mine = sum(after(small_way, qkv_cut))
    small_cut = [
        lax.dynamic_slice_in_dim(small_mine, (ctx_index ^ mask) * small_rows, small_rows, 0)
        for mask in range(parts)
    ]
    small_line_own = ctx_exchange(small_cut)
    out_cut = sum_and_pick(after(out_way, small_cut), parts, ctx_index)
    out_line_own = ctx_exchange(out_cut)
    down_own = total_of(after(down_way, out_cut))
    gate_own, up_own = unpick_units(after(pair_line_own, out_cut), groups_dp, ctx_index)
    _, normed_one_own, inverse_one_own = layer_norm(
        after(layer_input, out_cut).astype(jnp.float32), gain_one, shift_one
    )
    grad_norm_one = after(grad_norm_one, gate_own).astype(jnp.float32)
    grad_input = grad_mixed_own + norm_back(
        grad_norm_one, gain_one, normed_one_own, inverse_one_own
    )
    qkv_own = unpick_columns(after(qkv_line_own, gate_own), 3, ctx_index)
    small_own = sum(after(small_line_own, gate_own)).reshape(small_rows * LANES)
    out_own = unpick_columns(after(out_line_own, qkv_own), 1, ctx_index)
    feed_out = after(feed_out, qkv_own).astype(jnp.float32)
    layer_output = (mixed_own + feed_out).astype(jnp.bfloat16)
    return (
        layer_output,
        grad_input,
        small_own[:rows_here],
        small_own[rows_here : 2 * rows_here],
        qkv_own,
        small_own[4 * rows_here : 4 * rows_here + bias_here],
        out_own,
        small_own[2 * rows_here : 3 * rows_here],
        small_own[3 * rows_here : 4 * rows_here],
        gate_own,
        up_own,
        down_own,
    )


def solution(mesh):
    return jax.shard_map(
        shards,
        mesh=mesh,
        in_specs=(
            P(("dp", "ctx"), None),
            P("dp", None),
            P(("dp", "ctx")),
            P(("dp", "ctx")),
            P(("dp", "ctx")),
            P(("dp", "ctx"), None),
            P(("dp", "ctx")),
            P(("dp", "ctx"), None),
            P(("dp", "ctx")),
            P(("dp", "ctx")),
            P(("dp", "ctx"), None),
            P(("dp", "ctx"), None),
            P(("dp", "ctx"), None),
            P(("dp", "ctx"), None),
        ),
        out_specs=(
            P(("dp", "ctx"), None),
            P(("dp", "ctx"), None),
            P(("dp", "ctx")),
            P(("dp", "ctx")),
            P(("dp", "ctx"), None),
            P(("dp", "ctx")),
            P(("dp", "ctx"), None),
            P(("dp", "ctx")),
            P(("dp", "ctx")),
            P(("dp", "ctx"), None),
            P(("dp", "ctx"), None),
            P(("dp", "ctx"), None),
        ),
        check_vma=False,
    )
```
